512 devices in a mesh: dp: 16 (over y, x), vocab: 32 (over z, core).
Axes of the slice: x: 4, y: 4, z: 16, core: 2. Of those that a mesh axis runs over, the one named last changes fastest.
Arguments:
- hidden: bfloat16 [16384, 5120], P('dp', 'vocab'), may hold values from -6 to 6
- logit_grad: bfloat16 [16384, 6144], P('dp', 'vocab'), may hold values from -0.3984375 to 0.3984375
- predict_mask: int32 [16384], P('dp'), may hold values 0 or 1
- slot_grads: bfloat16 [512, 32, 6, 5120], P(('dp', 'vocab')), may hold values from -6 to 6
- slot_rows: int32 [512, 32, 6], P(('dp', 'vocab')), may hold values from 0 to 191
- slot_counts: int32 [512, 32], P(('dp', 'vocab')), may hold values from 0 to 6, as said below
- master: float32 [6144, 5120], P(('vocab', 'dp')), may hold values from -0.1 to 0.1
- first_moment: float32 [6144, 5120], P(('vocab', 'dp')), may hold values from -2 to 2
- second_moment: float32 [6144, 5120], P(('vocab', 'dp')), may hold values from 0.5 to 8
Outputs:
- master_new: float32 [6144, 5120], P(('vocab', 'dp'))
- first_new: float32 [6144, 5120], P(('vocab', 'dp'))
- second_new: float32 [6144, 5120], P(('vocab', 'dp'))
- table_new: bfloat16 [6144, 5120], P('vocab')
The draws below stay inside these ranges and needn't reach their ends.
Inputs may be any that keep to these rules, and one draw needn't show every extreme that they name: `slot_counts`: some owner receives 6 live slots from every sender, in every draw.
All inputs are finite; a program needn't handle non-finite values. No bound on the sum of `predict_mask` on one device may be relied on, other than what follows from the above.
Results may differ from the reference program's by a relative error of at most 0.0004.
Values may be sent and summed in bfloat16 or wider, within the bound.
A program may use at most 64 MiB of HBM per device.

```python
import math
import jax
import jax.numpy as jnp
import numpy as np
from jax import lax

D = 5120
CAP = 6
STEP = 8
ROWS_V = 192
W_ROWS = 6144
TOKENS_H = 16384
SENDERS = 512
OWNERS = 32


def draw_slot_counts(key, part):
    first_key, second_key = jax.random.split(jax.random.fold_in(key, 11))
    counts = jax.random.randint(first_key, (SENDERS, OWNERS), 0, CAP + 1)
    chosen = jax.random.randint(second_key, (), 0, OWNERS)
    owner_index = jnp.arange(OWNERS)[None, :]
    return jnp.where(owner_index == chosen, CAP, counts).astype(jnp.int32)


def with_ends(result, key, low, largest):
    longest = result.shape.index(max(result.shape))
    spots = []
    for shift in (0, 1):
        where = [jax.random.randint(jax.random.fold_in(key, axis), (), 0, length) for axis, length in enumerate(result.shape)]
        where[longest] = (where[longest] + shift) % result.shape[longest]
        spots.append(tuple(where))
    return result.at[spots[0]].set(low).at[spots[1]].set(largest)


def raised(drawn, own_key, source, target, shards_of, factor):
    def block_of(dim):
        return (jnp.arange(drawn.shape[dim]) // (drawn.shape[dim] // shards_of)).reshape((-1,) + (1,) * (drawn.ndim - 1 - dim))

    one_side = jax.random.permutation(own_key, shards_of)[block_of(target)]
    second = (block_of(target) + shards_of // 2) % shards_of
    return jnp.where((block_of(source) == one_side) | (block_of(source) == second), factor * drawn, drawn)


def steps_of(stream_key, dims, cuts, low, largest):
    loudness = 1.0
    for axis_at, shards_of in cuts:
        draws = jax.random.uniform(jax.random.fold_in(jax.random.fold_in(stream_key, 6), axis_at), (shards_of,), jnp.float32, low / len(cuts), largest / len(cuts))
        loudness = loudness * jnp.repeat(jnp.exp(draws), dims[axis_at] // shards_of).reshape((-1,) + (1,) * (len(dims) - 1 - axis_at))
    return loudness


def rank_bounds(number_of, skew):
    loads = [(1 << 20) // math.isqrt(rank ** skew) + 1 for rank in range(1, number_of + 1)]
    scale = 1 + sum(loads) // (1 << 30)
    return np.cumsum(np.array([max(1, weight // scale) for weight in loads]))


def ranked_ids(key, extent, number_of, skew):
    listing = rank_bounds(number_of, skew)
    lot = jax.random.randint(jax.random.fold_in(key, 1), extent, 0, int(listing[number_of - 1]))
    grade = jnp.searchsorted(jnp.asarray(listing, jnp.int32), lot, side="right")
    return jax.random.permutation(jax.random.fold_in(key, 2), number_of)[grade].astype(jnp.int32)


def noise(rng, shape, deviation, bound, pieces=(), kind=jnp.bfloat16):
    loudness = steps_of(rng, shape, pieces, -0.22, 0.18) if pieces else 1.0
    array = jax.random.normal(rng, shape, jnp.float32) * deviation * loudness
    return jnp.minimum(jnp.maximum(array, -bound), bound).astype(kind)


def bell_draw_with(stream_key, shape, width, limit, pieces, heavy, kind=jnp.bfloat16):
    result = width * jax.random.normal(stream_key, shape, jnp.float32)
    if pieces:
        result = result * steps_of(stream_key, shape, pieces, -0.22, 0.18)
    return jnp.clip(raised(result, jax.random.fold_in(stream_key, 3), *heavy), -limit, limit).astype(kind)


def setup_inputs(seed: int = 0) -> dict:
    arg_keys = jax.random.split(jax.random.key(seed), 10)
    return {
        "hidden": noise(arg_keys[0], (TOKENS_H, D), 1.0, 6.0, ((0, 16), (1, 32))),
        "logit_grad": bell_draw_with(arg_keys[1], (TOKENS_H, W_ROWS), 0.05, 0.3984375, ((0, 16), (1, 32)), (0, 1, 32, 2.75)),
        "predict_mask": with_ends((jax.random.randint(arg_keys[2], (TOKENS_H,), 0, 4) < 3).astype(jnp.int32), jax.random.fold_in(arg_keys[2], 1), 0, 1),
        "slot_grads": noise(arg_keys[3], (SENDERS, OWNERS, CAP, D), 1.0, 6.0, ((0, 512),)),
        "slot_rows": with_ends(ranked_ids(arg_keys[4], (SENDERS, OWNERS, CAP), ROWS_V, 2), jax.random.fold_in(arg_keys[4], 3), 0, ROWS_V - 1).astype(jnp.int32),
        "slot_counts": draw_slot_counts(jax.random.fold_in(arg_keys[9], 71), 0),
        "master": noise(arg_keys[6], (W_ROWS, D), 0.02, 0.1, ((0, 512),), jnp.float32),
        "first_moment": noise(arg_keys[7], (W_ROWS, D), 0.3, 2.0, ((0, 512),), jnp.float32),
        "second_moment": jnp.clip(jnp.exp(math.log(8.0) - 2.7725887 * jax.random.uniform(arg_keys[8], (W_ROWS, D), jnp.float32) ** steps_of(arg_keys[8], (W_ROWS, D), ((0, 512),), -0.2, 0.2)), 0.5, 8.0),
    }


def reference(hidden, logit_grad, predict_mask, slot_grads, slot_rows, slot_counts, master, first_moment, second_moment):
    masked = logit_grad * predict_mask.astype(jnp.bfloat16)[:, None]
    head_grad = lax.dot_general(masked, hidden, (((0,), (0,)), ((), ())), preferred_element_type=jnp.float32)
    owner_base = (jnp.arange(OWNERS, dtype=jnp.int32) * ROWS_V)[:, None]
    slot_index = jnp.arange(CAP, dtype=jnp.int32)[None, :]

    def add_sender(carried, inputs):
        grads, rows_local, counts = inputs
        alive_slot = (slot_index < counts[:, None]).astype(jnp.float32)
        values = grads.astype(jnp.float32) * alive_slot[:, :, None]
        targets = (rows_local + owner_base).astype(jnp.int32).reshape(-1)
        carried = carried.at[targets].add(values.reshape(-1, values.shape[-1]))
        return (carried, None)
    start_grad = jnp.zeros((W_ROWS, hidden.shape[1]), jnp.float32)
    embed_grad, unused = lax.scan(add_sender, start_grad, (slot_grads, slot_rows, slot_counts))
    gradient = head_grad + embed_grad
    first_new = 0.9 * first_moment + 0.1 * gradient
    second_new = 0.95 * second_moment + 0.05 * gradient * gradient
    first_hat = first_new / (1.0 - 0.9 ** STEP)
    second_hat = second_new / (1.0 - 0.95 ** STEP)
    master_new = master - 0.05 * (first_hat / (jnp.sqrt(second_hat) + 1e-08) + 0.1 * master)
    table_new = master_new.astype(jnp.bfloat16)
    return (master_new, first_new, second_new, table_new)
```

```python
import jax
import jax.numpy as jnp
from jax import lax
from jax.experimental import pallas as pl
from jax.experimental.pallas import tpu as pltpu
from jax.sharding import PartitionSpec as P

STEP = 8
Z = 16
NX = 4
NY = 4
DP = NX * NY
COLS = 640
NB = 8
UNITS = 48
PARTS = 4
PU = UNITS // PARTS
MESH = pl.DeviceIdType.MESH
F32 = jnp.float32
BF16 = jnp.bfloat16


def kernel(
    hid, logit, mask, slots, ids, master, first, second,
    master_o, first_o, second_o, table,
    hall, masked, outbox, inbox, part, ring, head, r1, q, r2, grad, emb,
    ag_s, ag_r, sib_s, sib_r, sl_s, sl_r, z_s, z_r,
    r1_s, r1_r, r2_s, r2_r, e_s, e_r, t1_s, t1_r, t2_s, t2_r, loc,
):
    d = lax.axis_index("dp")
    v = lax.axis_index("vocab")
    z, c = v // 2, v % 2
    y, x = d // NX, d % NX
    pg, h = d // 2, d % 2
    me = d * 2 + c

    def rc(src, dst, ss, rs, dev):
        return pltpu.make_async_remote_copy(
            src_ref=src, dst_ref=dst, send_sem=ss, recv_sem=rs,
            device_id=dev, device_id_type=MESH)

    up = (d, (v + 2) % 32)
    down = (d, (v + 30) % 32)
    sib = (d, z * 2 + (1 - c))
    zdir = (d, (v + 2 + 28 * c) % 32)

    bar = pltpu.get_barrier_semaphore()
    pl.semaphore_signal(bar, inc=1, device_id=up, device_id_type=MESH)
    pl.semaphore_signal(bar, inc=1, device_id=down, device_id_type=MESH)

    def greet(k, carry):
        o = (me + k) % 32
        pl.semaphore_signal(bar, inc=1, device_id=(o // 2, z * 2 + o % 2), device_id_type=MESH)
        return carry

    lax.fori_loop(1, 32, greet, 0)
    pl.semaphore_wait(bar, 33)

    def plane_at(sg, s):
        return (z - s + 16) % 16 if sg == 0 else (z + s) % 16

    def ag(sg, s, half):
        idx = plane_at(sg, s - 1) * 2 + c
        rows = pl.ds(80 * half, 80)
        ref = hall.at[idx, rows]
        src = hid.at[rows] if s == 1 else ref
        return rc(src, ref, ag_s.at[sg, s, half], ag_r.at[sg, s, half], up if sg == 0 else down)

    def ag_arrival(sg, s, half):
        idx = plane_at(sg, s) * 2 + c
        ref = hall.at[idx, pl.ds(80 * half, 80)]
        rc(ref, ref, ag_s.at[sg, s, half], ag_r.at[sg, s, half], up).wait_recv()

    def share(sg, s, half):
        idx = plane_at(sg, s) * 2 + c
        ref = hall.at[idx, pl.ds(80 * half, 80)]
        return rc(ref, ref, sib_s.at[sg, s, half], sib_r.at[sg, s, half], sib)

    def share_arrival(sg, s, half):
        idx = plane_at(sg, s) * 2 + 1 - c
        ref = hall.at[idx, pl.ds(80 * half, 80)]
        rc(ref, ref, sib_s.at[sg, s, half], sib_r.at[sg, s, half], sib).wait_recv()

    own_share = rc(hid, hall.at[v], sib_s.at[0, 0, 0], sib_r.at[0, 0, 0], sib)
    for half in (0, 1):
        ag(0, 1, half).start()
        ag(1, 1, half).start()
    own_share.start()
    own_copy = pltpu.make_async_copy(hid, hall.at[v], loc.at[0])
    own_copy.start()

    r = lax.broadcasted_iota(jnp.int32, (256, 224), 0)
    k = lax.broadcasted_iota(jnp.int32, (256, 224), 1)
    e = r % 8
    i = (r // 8) % 8
    to_plane = jnp.where((r // 64) % 2 == 0, z + 24 - i, z + 9 + i) % 16
    owner = to_plane * 2 + r // 128
    want = jnp.where(e < 6, e * 32 + owner, jnp.where(e == 6, 192 + owner, -1))
    select = jnp.where(want == k, 1.0, 0.0).astype(BF16)

    def slot_copy(g, w):
        to = (2 * g + w // 2, z * 2 + w % 2)
        return rc(outbox.at[g, w], inbox.at[me], sl_s.at[g * 4 + w], sl_r.at[me], to)

    def send_slots(g, carry):
        cols = pl.ds(pl.multiple_of(g * COLS, 128), COLS)
        rows = jnp.dot(select[:, :192], slots[:, cols], preferred_element_type=F32)
        rows = rows + jnp.dot(select[:, 192:], ids[...], preferred_element_type=F32)
        outbox[g] = rows.astype(BF16).reshape(4, 64, COLS)
        for w in range(4):
            mine = (2 * g + w // 2 == d) & (w % 2 == c)

            @pl.when(mine)
            def _():
                pltpu.make_async_copy(outbox.at[g, w], inbox.at[me], sl_r.at[me]).start()

            @pl.when(jnp.logical_not(mine))
            def _():
                slot_copy(g, w).start()
        return carry

    lax.fori_loop(0, NB, send_slots, 0)
    masked[...] = logit[...] * mask[...].astype(BF16)

    kz = z // 2

    def block_of(n):
        t = (n + 1) // 2
        return (kz + 16 + jnp.where(n % 2 == 1, -t, t)) % NB

    def stage1(n, g, xfirst):
        if xfirst:
            return rc(head.at[n, :, g], r1.at[n, x], r1_s.at[n, g], r1_r.at[n, x], (y * NX + g, v))
        return rc(head.at[n, g], r1.at[n, y], r1_s.at[n, g], r1_r.at[n, y], (g * NX + x, v))

    def stage2(n, g, xfirst):
        if xfirst:
            return rc(q.at[n, g], r2.at[n, y], r2_s.at[n, g], r2_r.at[n, y], (g * NX + x, v))
        return rc(q.at[n, g], r2.at[n, x], r2_s.at[n, g], r2_r.at[n, x], (y * NX + g, v))

    def head_block(n, xfirst):
        kb = block_of(n)
        rows = hall[pl.ds(4 * kb, 4)].reshape(COLS, 1024)
        val = lax.dot_general(masked[...], rows, (((1,), (1,)), ((), ())), preferred_element_type=F32)
        head[n] = val.reshape(NY, NX, 3, 4, COLS)
        mine = x if xfirst else y
        for o in range(1, 4):
            stage1(n, (mine + o) % 4, xfirst).start()

    def head_mid(n, xfirst):
        mine = x if xfirst else y
        for o in range(1, 4):
            src = (mine + o) % 4
            ref = r1.at[n, src]
            rc(ref, ref, r1_s.at[n, src], r1_r.at[n, src], up).wait_recv()
        own = head[n, :, x] if xfirst else head[n, y]
        q[n] = own + r1[n, (mine + 1) % 4] + r1[n, (mine + 2) % 4] + r1[n, (mine + 3) % 4]
        then = y if xfirst else x
        for o in range(1, 4):
            stage2(n, (then + o) % 4, xfirst).start()

    def head_end(n, xfirst):
        then = y if xfirst else x
        for o in range(1, 4):
            src = (then + o) % 4
            ref = r2.at[n, src]
            rc(ref, ref, r2_s.at[n, src], r2_r.at[n, src], up).wait_recv()
        grad[block_of(n)] = (
            q[n, then] + r2[n, (then + 1) % 4] + r2[n, (then + 2) % 4] + r2[n, (then + 3) % 4]
        )

    def ag_step(s):
        for half in (0, 1):
            for sg in (0, 1):
                if s == 8 and half != sg:
                    continue
                ag_arrival(sg, s, half)
                if s < 7 or (s == 7 and half == sg):
                    ag(sg, s + 1, half).start()
                share(sg, s, half).start()

    def shares_of(s):
        for half in (0, 1):
            for sg in (0, 1):
                if s == 8 and half != sg:
                    continue
                share_arrival(sg, s, half)

    def embed_parts():
        def arrived(s, carry):
            rc(inbox.at[s], inbox.at[s], sl_s.at[s], sl_r.at[s], up).wait_recv()
            return carry

        lax.fori_loop(0, 32, arrived, 0)

        def pair(p, carry):
            rows = inbox[:, pl.ds(pl.multiple_of(16 * p, 16), 16), :]
            tags = rows[:, :, :512].astype(F32)
            sub = lax.broadcasted_iota(jnp.int32, (32, 16, 512), 1)
            tags = jnp.where(sub % 8 == 6, tags, 0.0)
            tags = jnp.sum(jnp.sum(tags, axis=0), axis=0, keepdims=True)
            lane = lax.broadcasted_iota(jnp.int32, (1, 512), 1)
            shift = jnp.where((lane // 8) % 2 == 1, 192.0, 0.0)
            tags = jnp.where(tags > 0.5, tags + shift, 0.0)
            row = lax.broadcasted_iota(jnp.int32, (384, 512), 0).astype(F32) + 1.0
            hot = jnp.where(row == tags, 1.0, 0.0).astype(BF16)
            val = jnp.dot(hot, rows.reshape(512, COLS), preferred_element_type=F32)
            part[pl.ds(2 * p, 2)] = val.reshape(2, UNITS, 4, COLS)
            return carry

        lax.fori_loop(0, 4, pair, 0)

    def z_copy(s, src, p):
        rows = pl.ds(p * PU, PU)
        return rc(src.at[rows], ring.at[s, rows], z_s.at[s, p], z_r.at[s, p], zdir)

    def z_arrival(s, p):
        ref = ring.at[s, pl.ds(p * PU, PU)]
        rc(ref, ref, z_s.at[s, p], z_r.at[s, p], zdir).wait_recv()

    def z_step(s):
        for p in range(PARTS):
            if s == 0:
                z_copy(0, part.at[0], p).start()
                continue
            z_arrival(s - 1, p)
            rows = pl.ds(p * PU, PU)
            ring[s - 1, rows] = ring[s - 1, rows] + part[s, rows]
            if s < 7:
                z_copy(s, ring.at[s - 1], p).start()
            else:

                @pl.when(c == 0)
                def _():
                    z_copy(s, ring.at[s - 1], p).start()

    own_copy.wait()
    ag_step(1)
    ag_step(2)
    own_idx = v + 1 - 2 * c
    rc(hid, hall.at[own_idx], sib_s.at[0, 0, 0], sib_r.at[0, 0, 0], sib).wait_recv()
    shares_of(1)
    head_block(0, True)
    ag_step(3)
    shares_of(2)
    shares_of(3)
    head_block(1, False)
    ag_step(4)
    head_block(2, True)
    head_mid(0, True)
    ag_step(5)
    shares_of(4)
    shares_of(5)
    head_block(3, False)
    ag_step(6)
    head_block(4, True)
    embed_parts()
    ag_step(7)
    z_step(0)
    head_mid(1, False)
    head_mid(2, True)
    ag_step(8)
    shares_of(6)
    shares_of(7)
    z_step(1)
    head_block(5, False)
    z_step(2)
    head_block(6, True)
    z_step(3)
    shares_of(8)
    head_block(7, False)
    z_step(4)
    head_mid(3, False)
    head_mid(4, True)
    z_step(5)
    head_mid(5, False)
    head_mid(6, True)
    z_step(6)
    head_mid(7, False)
    for n in range(5):
        head_end(n, n % 2 == 0)
    z_step(7)
    for n in range(5, 8):
        head_end(n, n % 2 == 0)

    fin = 7 - c

    def e_copy(t):
        return rc(ring.at[fin, pl.ds(3 * t, 3)], emb.at[c, pg], e_s.at[t], e_r.at[c, pg], (t, z * 2 + h))

    for p in range(PARTS):

        @pl.when(c == 0)
        def _():
            z_arrival(7, p)

        for t in range(4 * p, 4 * p + 4):
            mine = (t == d) & (h == c)

            @pl.when(mine)
            def _():
                pltpu.make_async_copy(
                    ring.at[fin, pl.ds(3 * t, 3)], emb.at[c, pg], e_r.at[c, pg]).start()

            @pl.when(jnp.logical_not(mine))
            def _():
                e_copy(t).start()

    corr1 = 1.0 / (1.0 - 0.9**STEP)
    corr2 = 1.0 / (1.0 - 0.95**STEP)
    for b in range(NB):
        for w in (0, 1):
            ref = emb.at[w, b]
            rc(ref, ref, e_s.at[b], e_r.at[w, b], up).wait_recv()
        g = grad[b] + emb[0, b] + emb[1, b]
        g = jnp.concatenate([g[0], g[1], g[2]], axis=0)
        cols = pl.ds(b * COLS, COLS)
        m = master[:, cols]
        fn = 0.9 * first[:, cols] + 0.1 * g
        sn = 0.95 * second[:, cols] + 0.05 * g * g
        mn = m - 0.05 * (fn * corr1 / (jnp.sqrt(sn * corr2) + 1e-08) + 0.1 * m)
        first_o[:, cols] = fn
        second_o[:, cols] = sn
        master_o[:, cols] = mn
        table[y, x, b // 4, :, pl.ds((b % 4) * COLS, COLS)] = mn.astype(BF16)

    def t1(w, g):
        ref = table.at[y, x, w]
        to = (y * NX + g, v) if w == 0 else (g * NX + x, v)
        return rc(ref, ref, t1_s.at[w, g], t1_r.at[w, x if w == 0 else y], to)

    def t1_arrival(w, g):
        ref = table.at[y, g, w] if w == 0 else table.at[g, x, w]
        rc(ref, ref, t1_s.at[w, g], t1_r.at[w, g], up).wait_recv()

    def t2(w, g):
        if w == 0:
            ref, to, i = table.at[y, :, w], (g * NX + x, v), y
        else:
            ref, to, i = table.at[:, x, w], (y * NX + g, v), x
        return rc(ref, ref, t2_s.at[w, g], t2_r.at[w, i], to)

    def t2_arrival(w, g):
        ref = table.at[g, :, w] if w == 0 else table.at[:, g, w]
        rc(ref, ref, t2_s.at[w, g], t2_r.at[w, g], up).wait_recv()

    firsts = (x, y)
    seconds = (y, x)
    for o in range(1, 4):
        for w in (0, 1):
            t1(w, (firsts[w] + o) % 4).start()
    for w in (0, 1):
        for o in range(1, 4):
            t1_arrival(w, (firsts[w] + o) % 4)
        for o in range(1, 4):
            t2(w, (seconds[w] + o) % 4).start()
    for w in (0, 1):
        for o in range(1, 4):
            t2_arrival(w, (seconds[w] + o) % 4)

    own_share.wait_send()
    for s in range(1, 9):
        for half in (0, 1):
            for sg in (0, 1):
                if s == 8 and half != sg:
                    continue
                ag(sg, s, half).wait_send()
                share(sg, s, half).wait_send()

    def slots_left(g, carry):
        for w in range(4):

            @pl.when(jnp.logical_not((2 * g + w // 2 == d) & (w % 2 == c)))
            def _():
                slot_copy(g, w).wait_send()
        return carry

    lax.fori_loop(0, NB, slots_left, 0)
    for n in range(NB):
        xfirst = n % 2 == 0
        for o in range(1, 4):
            stage1(n, ((x if xfirst else y) + o) % 4, xfirst).wait_send()
            stage2(n, ((y if xfirst else x) + o) % 4, xfirst).wait_send()
    for s in range(8):
        for p in range(PARTS):
            src = part.at[0] if s == 0 else ring.at[s - 1]
            if s < 7:
                z_copy(s, src, p).wait_send()
            else:

                @pl.when(c == 0)
                def _():
                    z_copy(s, src, p).wait_send()
    for t in range(DP):

        @pl.when(jnp.logical_not((t == d) & (h == c)))
        def _():
            e_copy(t).wait_send()
    for w in (0, 1):
        for o in range(1, 4):
            t1(w, (firsts[w] + o) % 4).wait_send()
            t2(w, (seconds[w] + o) % 4).wait_send()


def local(hidden, logit_grad, predict_mask, slot_grads, slot_rows, slot_counts, master, first, second):
    me = lax.axis_index("dp") * 2 + lax.axis_index("vocab") % 2
    live = jnp.arange(6, dtype=jnp.int32)[None, :] < slot_counts[0][:, None]
    tag = jnp.where(live, slot_rows[0] + 1, 0).astype(BF16)
    lane = jnp.arange(COLS, dtype=jnp.int32)
    wide = jnp.pad(tag, ((0, 0), (0, 2)))
    wide = jnp.tile(wide, (1, COLS // 8))
    ids = jnp.where((lane // 16 == me)[None, :], wide, jnp.zeros((), BF16))
    z = lax.axis_index("vocab") // 2
    plane = jnp.arange(32, dtype=jnp.int32) // 2
    rel = (plane - z - 1) % 16
    step = jnp.where(rel < 8, 7 - rel, rel - 8)
    ids = jnp.where((lane[None, :] // 8) % 2 == (step % 2)[:, None], ids, jnp.zeros((), BF16))
    slots = slot_grads[0].transpose(1, 0, 2).reshape(192, 5120)
    vm = pl.BlockSpec(memory_space=pltpu.VMEM)
    dma = pltpu.SemaphoreType.DMA
    out = pl.pallas_call(
        kernel,
        out_shape=(
            jax.ShapeDtypeStruct((12, 5120), F32),
            jax.ShapeDtypeStruct((12, 5120), F32),
            jax.ShapeDtypeStruct((12, 5120), F32),
            jax.ShapeDtypeStruct((NY, NX, 2, 12, 2560), BF16),
        ),
        in_specs=[vm] * 8,
        out_specs=(vm,) * 4,
        scratch_shapes=[
            pltpu.VMEM((32, 160, 1024), BF16),
            pltpu.VMEM((192, 1024), BF16),
            pltpu.VMEM((NB, 4, 64, COLS), BF16),
            pltpu.VMEM((32, 64, COLS), BF16),
            pltpu.VMEM((8, UNITS, 4, COLS), F32),
            pltpu.VMEM((8, UNITS, 4, COLS), F32),
            pltpu.VMEM((NB, NY, NX, 3, 4, COLS), F32),
            pltpu.VMEM((NB, 4, 4, 3, 4, COLS), F32),
            pltpu.VMEM((NB, 4, 3, 4, COLS), F32),
            pltpu.VMEM((NB, 4, 3, 4, COLS), F32),
            pltpu.VMEM((NB, 3, 4, COLS), F32),
            pltpu.VMEM((2, NB, 3, 4, COLS), F32),
            dma((2, 9, 2)), dma((2, 9, 2)), dma((2, 9, 2)), dma((2, 9, 2)),
            dma((32,)), dma((32,)), dma((8, PARTS)), dma((8, PARTS)),
            dma((NB, 4)), dma((NB, 4)), dma((NB, 4)), dma((NB, 4)),
            dma((DP,)), dma((2, NB)),
            dma((2, 4)), dma((2, 4)), dma((2, 4)), dma((2, 4)),
            dma((1,)),
        ],
        compiler_params=pltpu.CompilerParams(
            collective_id=0, has_side_effects=True, vmem_limit_bytes=60 * 1024 * 1024),
    )(hidden.T, logit_grad.T, predict_mask[None, :], slots, ids, master, first, second)
    table = out[3].transpose(0, 1, 3, 2, 4).reshape(192, 5120)
    return out[0], out[1], out[2], table


def solution(mesh):
    in_specs = (
        P("dp", "vocab"),
        P("dp", "vocab"),
        P("dp"),
        P(("dp", "vocab"), None, None, None),
        P(("dp", "vocab"), None, None),
        P(("dp", "vocab"), None),
        P(("vocab", "dp"), None),
        P(("vocab", "dp"), None),
        P(("vocab", "dp"), None),
    )
    out_specs = (
        P(("vocab", "dp"), None),
        P(("vocab", "dp"), None),
        P(("vocab", "dp"), None),
        P("vocab", None),
    )
    return jax.shard_map(local, mesh=mesh, in_specs=in_specs, out_specs=out_specs, check_vma=False)
```

```python
import jax
import jax.numpy as jnp
from jax import lax
from jax.experimental import pallas as pl
from jax.experimental.pallas import tpu as pltpu
from jax.sharding import PartitionSpec as P

STEP = 8
Z = 16
NX = 4
NY = 4
DP = NX * NY
COLS = 640
NB = 8
UNITS = 48
PARTS = 4
PU = UNITS // PARTS
HALF = ((0, 384), (384, 256))
MESH = pl.DeviceIdType.MESH
F32 = jnp.float32
BF16 = jnp.bfloat16


def update(g, m, mu, nu):
    fn = 0.9 * mu + 0.1 * g
    sn = 0.95 * nu + 0.05 * g * g
    corr1 = 1.0 / (1.0 - 0.9**STEP)
    corr2 = 1.0 / (1.0 - 0.95**STEP)
    mn = m - 0.05 * (fn * corr1 / (jnp.sqrt(sn * corr2) + 1e-08) + 0.1 * m)
    return mn, fn, sn


def kernel(
    hid, logit, mask, slots, rows_in, counts, master, first, second,
    grad_o, table,
    hall, masked, outbox, inbox, part0, part1, ring0, ring1, head, ra, r1, q, r2, grad, emb0, emb1, tags_v, ta, tb,
    ag_s, ag_r, sib_s, sib_r, sl_s, sl_r, z_s, z_r,
    ra_s, ra_r, r1_s, r1_r, r2_s, r2_r, e_s, e_r, t1_s, t1_r, t2_s, t2_r, t3_s, t3_r, loc,
):
    d = lax.axis_index("dp")
    v = lax.axis_index("vocab")
    z, c = v // 2, v % 2
    y, x = d // NX, d % NX
    pg, h = d // 2, d % 2
    me = d * 2 + c

    def rc(src, dst, ss, rs, dev):
        return pltpu.make_async_remote_copy(
            src_ref=src, dst_ref=dst, send_sem=ss, recv_sem=rs,
            device_id=dev, device_id_type=MESH)

    up = (d, (v + 2) % 32)
    down = (d, (v + 30) % 32)
    sib = (d, z * 2 + (1 - c))
    zdir = (d, (v + 2 + 28 * c) % 32)

    bar = pltpu.get_barrier_semaphore()
    pl.semaphore_signal(bar, inc=1, device_id=up, device_id_type=MESH)
    pl.semaphore_signal(bar, inc=1, device_id=down, device_id_type=MESH)

    def greet(k, carry):
        o = (me + k) % 32
        pl.semaphore_signal(bar, inc=1, device_id=(o // 2, z * 2 + o % 2), device_id_type=MESH)
        return carry

    lax.fori_loop(1, 32, greet, 0)
    pl.semaphore_wait(bar, 33)

    def plane_at(sg, s):
        return (z - s + 16) % 16 if sg == 0 else (z + s) % 16

    def ag(sg, s, half):
        idx = plane_at(sg, s - 1) * 2 + c
        rows = pl.ds(80 * half, 80)
        ref = hall.at[idx, rows]
        src = hid.at[rows] if s == 1 else ref
        return rc(src, ref, ag_s.at[sg, s, half], ag_r.at[sg, s, half], up if sg == 0 else down)

    def ag_arrival(sg, s, half):
        idx = plane_at(sg, s) * 2 + c
        ref = hall.at[idx, pl.ds(80 * half, 80)]
        rc(ref, ref, ag_s.at[sg, s, half], ag_r.at[sg, s, half], up).wait_recv()

    def share(sg, s, half):
        idx = plane_at(sg, s) * 2 + c
        ref = hall.at[idx, pl.ds(80 * half, 80)]
        return rc(ref, ref, sib_s.at[sg, s, half], sib_r.at[sg, s, half], sib)

    def share_arrival(sg, s, half):
        idx = plane_at(sg, s) * 2 + 1 - c
        ref = hall.at[idx, pl.ds(80 * half, 80)]
        rc(ref, ref, sib_s.at[sg, s, half], sib_r.at[sg, s, half], sib).wait_recv()

    own_share = rc(hid, hall.at[v], sib_s.at[0, 0, 0], sib_r.at[0, 0, 0], sib)
    for half in (0, 1):
        ag(0, 1, half).start()
        ag(1, 1, half).start()
    own_share.start()
    own_copy = pltpu.make_async_copy(hid, hall.at[v], loc.at[0])
    own_copy.start()

    part, ring, emb, rowsets = (part0, part1), (ring0, ring1), (emb0, emb1), (ta, tb)

    def row_maps(width):
        r = lax.broadcasted_iota(jnp.int32, (256, width), 0)
        k = lax.broadcasted_iota(jnp.int32, (256, width), 1)
        i = (r // 8) % 8
        to_plane = jnp.where((r // 64) % 2 == 0, z + 24 - i, z + 9 + i) % 16
        return k, r % 8, i, to_plane * 2 + r // 128

    k, e, _, owner = row_maps(192)
    select = jnp.where((e < 6) & (e * 32 + owner == k), 1.0, 0.0).astype(BF16)
    k, e, _, owner = row_maps(32)
    pick = jnp.where((e == 6) & (owner == k), 1.0, 0.0).astype(BF16)
    live = lax.broadcasted_iota(jnp.int32, (6, 32), 0) < counts[...]
    tag = jnp.where(live, rows_in[:, 0, :] + 1, 0).astype(F32)
    tag = jnp.concatenate([tag, jnp.zeros((2, 32), F32)], axis=0).astype(BF16)
    tag = lax.dot_general(pick, tag, (((1,), (1,)), ((), ())), preferred_element_type=F32)
    a = lax.broadcasted_iota(jnp.int32, (8, COLS), 0)
    b = lax.broadcasted_iota(jnp.int32, (8, COLS), 1)
    spread = jnp.where((b % 8 == a) & (b // 16 == me), 1.0, 0.0).astype(BF16)
    tag = jnp.dot(tag.astype(BF16), spread, preferred_element_type=F32)
    k, _, i, _ = row_maps(COLS)
    tags_v[...] = jnp.where((k // 8) % 2 == i % 2, tag, 0.0)

    def slot_copy(g, w):
        to = (2 * g + w // 2, z * 2 + w % 2)
        return rc(outbox.at[g, w], inbox.at[me], sl_s.at[g * 4 + w], sl_r.at[me], to)

    def send_slots(g, carry):
        cols = pl.ds(pl.multiple_of(g * COLS, 128), COLS)
        rows = jnp.dot(select, slots[:, cols], preferred_element_type=F32) + tags_v[...]
        outbox[g] = rows.astype(BF16).reshape(4, 64, COLS)
        for w in range(4):
            mine = (2 * g + w // 2 == d) & (w % 2 == c)

            @pl.when(mine)
            def _():
                pltpu.make_async_copy(outbox.at[g, w], inbox.at[me], sl_r.at[me]).start()

            @pl.when(jnp.logical_not(mine))
            def _():
                slot_copy(g, w).start()
        return carry

    lax.fori_loop(0, 2, send_slots, 0)
    kz = z // 2

    def block_of(n):
        t = (n + 1) // 2
        return (kz + 16 + jnp.where(n % 2 == 1, -t, t)) % NB

    def at_axis(g, xfirst):
        return (y * NX + g, v) if xfirst else (g * NX + x, v)

    def stage0(n, side, xfirst):
        mine = x if xfirst else y
        opp, to = (mine + 2) % 4, (mine + 1 + 2 * side) % 4
        rows = pl.ds(2 * side, 2)
        ref = head.at[n, rows, opp] if xfirst else head.at[n, opp, rows]
        return rc(ref, ra.at[n, side], ra_s.at[n, side], ra_r.at[n, side], at_axis(to, xfirst))

    def stage1(n, side, xfirst):
        to = ((x if xfirst else y) + 1 + 2 * side) % 4
        ref = head.at[n, :, to] if xfirst else head.at[n, to]
        return rc(ref, r1.at[n, side], r1_s.at[n, side], r1_r.at[n, side], at_axis(to, xfirst))

    def stage2(n, g, xfirst):
        if xfirst:
            return rc(q.at[n, g], r2.at[n, y], r2_s.at[n, g], r2_r.at[n, y], (g * NX + x, v))
        return rc(q.at[n, g], r2.at[n, x], r2_s.at[n, g], r2_r.at[n, x], (y * NX + g, v))

    def head_block(n):
        kb = block_of(n)
        rows = hall[pl.ds(4 * kb, 4)].reshape(COLS, 1024)
        val = lax.dot_general(masked[...], rows, (((1,), (1,)), ((), ())), preferred_element_type=F32)
        head[n] = val.reshape(NY, NX, 3, 4, COLS)

    def head_send(n):
        for side in (0, 1):
            stage0(n, side, n % 2 == 0).start()

    def head_add(n):
        xfirst = n % 2 == 0
        mine = x if xfirst else y
        for side in (0, 1):
            ref = ra.at[n, side]
            rc(ref, ref, ra_s.at[n, side], ra_r.at[n, side], up).wait_recv()
            to = (mine + 1 + 2 * side) % 4
            rows = pl.ds(2 * side, 2)
            if xfirst:
                head[n, rows, to] = head[n, rows, to] + ra[n, side]
            else:
                head[n, to, rows] = head[n, to, rows] + ra[n, side]
            stage1(n, side, xfirst).start()

    def head_mid(n):
        xfirst = n % 2 == 0
        for side in (0, 1):
            ref = r1.at[n, side]
            rc(ref, ref, r1_s.at[n, side], r1_r.at[n, side], up).wait_recv()
        own = head[n, :, x] if xfirst else head[n, y]
        q[n] = own + r1[n, 0] + r1[n, 1]
        then = y if xfirst else x
        for o in range(1, 4):
            stage2(n, (then + o) % 4, xfirst).start()

    def head_end(n):
        xfirst = n % 2 == 0
        then = y if xfirst else x
        for o in range(1, 4):
            src = (then + o) % 4
            ref = r2.at[n, src]
            rc(ref, ref, r2_s.at[n, src], r2_r.at[n, src], up).wait_recv()
        grad[block_of(n)] = (
            q[n, then] + r2[n, (then + 1) % 4] + r2[n, (then + 2) % 4] + r2[n, (then + 3) % 4]
        )

    def ag_step(s):
        for half in (0, 1):
            for sg in (0, 1):
                if s == 8 and half != sg:
                    continue
                ag_arrival(sg, s, half)
                if s < 7 or (s == 7 and half == sg):
                    ag(sg, s + 1, half).start()
                share(sg, s, half).start()

    def shares_of(s):
        for half in (0, 1):
            for sg in (0, 1):
                if s == 8 and half != sg:
                    continue
                share_arrival(sg, s, half)

    def embed_parts():
        def arrived(s, carry):
            rc(inbox.at[s], inbox.at[s], sl_s.at[s], sl_r.at[s], up).wait_recv()
            return carry

        lax.fori_loop(0, 32, arrived, 0)

        def pair(p, carry):
            rows = inbox[:, pl.ds(pl.multiple_of(16 * p, 16), 16), :]
            tags = rows[:, :, :512].astype(F32)
            sub = lax.broadcasted_iota(jnp.int32, (32, 16, 512), 1)
            tags = jnp.where(sub % 8 == 6, tags, 0.0)
            tags = jnp.sum(jnp.sum(tags, axis=0), axis=0, keepdims=True)
            lane = lax.broadcasted_iota(jnp.int32, (1, 512), 1)
            shift = jnp.where((lane // 8) % 2 == 1, 192.0, 0.0)
            tags = jnp.where(tags > 0.5, tags + shift, 0.0)
            row = lax.broadcasted_iota(jnp.int32, (384, 512), 0).astype(F32) + 1.0
            hot = jnp.where(row == tags, 1.0, 0.0).astype(BF16)
            val = jnp.dot(hot, rows.reshape(512, COLS), preferred_element_type=F32)
            for a, (off, n) in enumerate(HALF):
                part[a][pl.ds(2 * p, 2)] = val[:, off:off + n].reshape(2, UNITS, 4, n)
            return carry

        lax.fori_loop(0, 4, pair, 0)

    def z_copy(s, src, p, a):
        rows = pl.ds(p * PU, PU)
        return rc(src.at[rows], ring[a].at[s, rows], z_s.at[a, s, p], z_r.at[a, s, p], zdir)

    def z_arrival(s, p, a):
        ref = ring[a].at[s, pl.ds(p * PU, PU)]
        rc(ref, ref, z_s.at[a, s, p], z_r.at[a, s, p], zdir).wait_recv()

    def z_step(s, a):
        for p in range(PARTS):
            if s == 0:
                z_copy(0, part[a].at[0], p, a).start()
                continue
            z_arrival(s - 1, p, a)
            rows = pl.ds(p * PU, PU)
            ring[a][s - 1, rows] = ring[a][s - 1, rows] + part[a][s, rows]
            if s < 7:
                z_copy(s, ring[a].at[s - 1], p, a).start()
            else:

                @pl.when(c == 0)
                def _():
                    z_copy(s, ring[a].at[s - 1], p, a).start()

    fin = 7 - c

    def e_refs(t, a):
        return ring[a].at[fin, pl.ds(3 * t, 3)], emb[a].at[c, pg]

    def e_copy(t, a):
        src, dst = e_refs(t, a)
        return rc(src, dst, e_s.at[a, t], e_r.at[a, c, pg], (t, z * 2 + h))

    def finish(a):
        for p in range(PARTS):

            @pl.when(c == 0)
            def _():
                z_arrival(7, p, a)

            for t in range(4 * p, 4 * p + 4):
                mine = (t == d) & (h == c)

                @pl.when(mine)
                def _():
                    src, dst = e_refs(t, a)
                    pltpu.make_async_copy(src, dst, e_r.at[a, c, pg]).start()

                @pl.when(jnp.logical_not(mine))
                def _():
                    e_copy(t, a).start()

    def adam(a):
        off, n = HALF[a]
        for b in range(NB):
            cut = pl.ds(off, n)
            for w in (0, 1):
                ref = emb[a].at[w, b]
                rc(ref, ref, e_s.at[a, b], e_r.at[a, w, b], up).wait_recv()
            g = grad[b, :, :, cut] + emb[a][0, b] + emb[a][1, b]
            g = jnp.concatenate([g[0], g[1], g[2]], axis=0)
            cols = pl.ds(b * COLS + off, n)
            mn, _, _ = update(g, master[:, cols], first[:, cols], second[:, cols])
            grad_o[:, cols] = g
            mn = mn.astype(BF16)
            for u in range(3):
                rowsets[a][b // 4, y, x, u, :, pl.ds((b % 4) * n, n)] = mn[4 * u:4 * u + 4]

    firsts = (x, y)
    seconds = (y, x)

    def group(a, w, g):
        return rowsets[a].at[w, g] if w == 0 else rowsets[a].at[w, :, g]

    def t1(a, w, g):
        ref = rowsets[a].at[w, y, x]
        to = (y * NX + g, v) if w == 0 else (g * NX + x, v)
        return rc(ref, ref, t1_s.at[a, w, g], t1_r.at[a, w, firsts[w]], to)

    def t2(a, w, side):
        ref = group(a, w, seconds[w])
        to = at_axis((seconds[w] + 1 + 2 * side) % 4, w == 1)
        return rc(ref, ref, t2_s.at[a, w, side], t2_r.at[a, w, side], to)

    def t3(a, w, side):
        g = (seconds[w] + 3 + 2 * side) % 4
        ref = group(a, w, g).at[pl.ds(2 * side, 2)]
        to = at_axis((seconds[w] + 1 + 2 * side) % 4, w == 1)
        return rc(ref, ref, t3_s.at[a, w, side], t3_r.at[a, w, side], to)

    def spread_rows(a):
        for o in range(1, 4):
            for w in (0, 1):
                t1(a, w, (firsts[w] + o) % 4).start()

    def spread_groups(a):
        for w in (0, 1):
            for o in range(1, 4):
                g = (firsts[w] + o) % 4
                ref = rowsets[a].at[w, y, g] if w == 0 else rowsets[a].at[w, g, x]
                rc(ref, ref, t1_s.at[a, w, g], t1_r.at[a, w, g], up).wait_recv()
            for side in (0, 1):
                t2(a, w, side).start()

    def pass_groups(a):
        for w in (0, 1):
            for side in (0, 1):
                ref = group(a, w, (seconds[w] + 3 + 2 * side) % 4)
                rc(ref, ref, t2_s.at[a, w, side], t2_r.at[a, w, side], up).wait_recv()
                t3(a, w, side).start()

    def gathered(a):
        for w in (0, 1):
            for side in (0, 1):
                ref = group(a, w, (seconds[w] + 2) % 4).at[pl.ds(2 * side, 2)]
                rc(ref, ref, t3_s.at[a, w, side], t3_r.at[a, w, side], up).wait_recv()

    def write_table(a):
        off, n = HALF[a]
        for w in (0, 1):
            for b in range(4):
                for m in range(12):
                    units = [4 * m + i for i in range(4)]
                    cut = pl.ds(b * n, n)
                    rows = [rowsets[a][w, t // 12, (t // 3) % 4, t % 3, :, cut] for t in units]
                    table[pl.ds(16 * m, 16), pl.ds((4 * w + b) * COLS + off, n)] = jnp.concatenate(rows, axis=0)

    own_copy.wait()
    ag_step(1)
    lax.fori_loop(2, 5, send_slots, 0)
    ag_step(2)
    lax.fori_loop(5, 8, send_slots, 0)
    own_idx = v + 1 - 2 * c
    rc(hid, hall.at[own_idx], sib_s.at[0, 0, 0], sib_r.at[0, 0, 0], sib).wait_recv()
    masked[...] = logit[...] * mask[...].astype(BF16)
    ag_step(3)
    shares_of(1)
    head_block(0)
    shares_of(2)
    shares_of(3)
    ag_step(4)
    head_block(1)
    head_block(2)
    ag_step(5)
    shares_of(4)
    shares_of(5)
    head_block(3)
    ag_step(6)
    head_block(4)
    ag_step(7)
    embed_parts()
    z_step(0, 0)
    for n in range(5):
        head_send(n)
    shares_of(6)
    shares_of(7)
    head_block(5)
    head_block(6)
    head_send(5)
    head_send(6)
    ag_step(8)
    z_step(1, 0)
    shares_of(8)
    head_block(7)
    head_send(7)
    head_add(0)
    head_add(1)
    z_step(2, 0)
    head_add(2)
    head_add(3)
    z_step(3, 0)
    head_mid(0)
    head_mid(1)
    head_add(4)
    z_step(4, 0)
    head_mid(2)
    head_mid(3)
    head_add(5)
    z_step(5, 0)
    head_mid(4)
    head_end(0)
    head_end(1)
    head_add(6)
    z_step(6, 0)
    z_step(0, 1)
    head_mid(5)
    head_end(2)
    head_end(3)
    head_add(7)
    z_step(7, 0)
    z_step(1, 1)
    finish(0)
    head_mid(6)
    head_end(4)
    z_step(2, 1)
    head_mid(7)
    head_end(5)
    z_step(3, 1)
    head_end(6)
    head_end(7)
    z_step(4, 1)
    adam(0)
    spread_rows(0)
    z_step(5, 1)
    z_step(6, 1)
    spread_groups(0)
    z_step(7, 1)
    finish(1)
    pass_groups(0)
    gathered(0)
    write_table(0)
    adam(1)
    spread_rows(1)
    spread_groups(1)
    pass_groups(1)
    gathered(1)
    write_table(1)

    own_share.wait_send()
    for s in range(1, 9):
        for half in (0, 1):
            for sg in (0, 1):
                if s == 8 and half != sg:
                    continue
                ag(sg, s, half).wait_send()
                share(sg, s, half).wait_send()

    def slots_left(g, carry):
        for w in range(4):

            @pl.when(jnp.logical_not((2 * g + w // 2 == d) & (w % 2 == c)))
            def _():
                slot_copy(g, w).wait_send()
        return carry

    lax.fori_loop(0, NB, slots_left, 0)
    for n in range(NB):
        xfirst = n % 2 == 0
        for side in (0, 1):
            stage0(n, side, xfirst).wait_send()
            stage1(n, side, xfirst).wait_send()
        for o in range(1, 4):
            stage2(n, ((y if xfirst else x) + o) % 4, xfirst).wait_send()
    for a in (0, 1):
        for s in range(8):
            for p in range(PARTS):
                src = part[a].at[0] if s == 0 else ring[a].at[s - 1]
                if s < 7:
                    z_copy(s, src, p, a).wait_send()
                else:

                    @pl.when(c == 0)
                    def _():
                        z_copy(s, src, p, a).wait_send()
        for t in range(DP):

            @pl.when(jnp.logical_not((t == d) & (h == c)))
            def _():
                e_copy(t, a).wait_send()
        for w in (0, 1):
            for o in range(1, 4):
                t1(a, w, (firsts[w] + o) % 4).wait_send()
            for side in (0, 1):
                t2(a, w, side).wait_send()
                t3(a, w, side).wait_send()


def local(hidden, logit_grad, predict_mask, slot_grads, slot_rows, slot_counts, master, first, second):
    slots = slot_grads[0].transpose(1, 0, 2).reshape(192, 5120)
    rows_in = slot_rows.transpose(2, 0, 1)
    vm = pl.BlockSpec(memory_space=pltpu.VMEM)
    dma = pltpu.SemaphoreType.DMA
    grad, table = pl.pallas_call(
        kernel,
        out_shape=(
            jax.ShapeDtypeStruct((12, 5120), F32),
            jax.ShapeDtypeStruct((192, 5120), BF16),
        ),
        in_specs=[vm] * 9,
        out_specs=(vm,) * 2,
        scratch_shapes=[
            pltpu.VMEM((32, 160, 1024), BF16),
            pltpu.VMEM((192, 1024), BF16),
            pltpu.VMEM((NB, 4, 64, COLS), BF16),
            pltpu.VMEM((32, 64, COLS), BF16),
            pltpu.VMEM((8, UNITS, 4, HALF[0][1]), F32),
            pltpu.VMEM((8, UNITS, 4, HALF[1][1]), F32),
            pltpu.VMEM((8, UNITS, 4, HALF[0][1]), F32),
            pltpu.VMEM((8, UNITS, 4, HALF[1][1]), F32),
            pltpu.VMEM((NB, NY, NX, 3, 4, COLS), F32),
            pltpu.VMEM((NB, 2, 2, 3, 4, COLS), F32),
            pltpu.VMEM((NB, 2, 4, 3, 4, COLS), F32),
            pltpu.VMEM((NB, 4, 3, 4, COLS), F32),
            pltpu.VMEM((NB, 4, 3, 4, COLS), F32),
            pltpu.VMEM((NB, 3, 4, COLS), F32),
            pltpu.VMEM((2, NB, 3, 4, HALF[0][1]), F32),
            pltpu.VMEM((2, NB, 3, 4, HALF[1][1]), F32),
            pltpu.VMEM((256, COLS), F32),
            pltpu.VMEM((2, NY, NX, 3, 4, 4 * HALF[0][1]), BF16),
            pltpu.VMEM((2, NY, NX, 3, 4, 4 * HALF[1][1]), BF16),
            dma((2, 9, 2)), dma((2, 9, 2)), dma((2, 9, 2)), dma((2, 9, 2)),
            dma((32,)), dma((32,)), dma((2, 8, PARTS)), dma((2, 8, PARTS)),
            dma((NB, 2)), dma((NB, 2)), dma((NB, 2)), dma((NB, 2)), dma((NB, 4)), dma((NB, 4)),
            dma((2, DP)), dma((2, 2, NB)),
            dma((2, 2, 4)), dma((2, 2, 4)), dma((2, 2, 2)), dma((2, 2, 2)), dma((2, 2, 2)), dma((2, 2, 2)),
            dma((1,)),
        ],
        compiler_params=pltpu.CompilerParams(
            collective_id=0, has_side_effects=True, vmem_limit_bytes=60 * 1024 * 1024),
    )(hidden.T, logit_grad.T, predict_mask[None, :], slots, rows_in, slot_counts, master, first, second)
    return (*update(grad, master, first, second), table)


def solution(mesh):
    in_specs = (
        P("dp", "vocab"),
        P("dp", "vocab"),
        P("dp"),
        P(("dp", "vocab"), None, None, None),
        P(("dp", "vocab"), None, None),
        P(("dp", "vocab"), None),
        P(("vocab", "dp"), None),
        P(("vocab", "dp"), None),
        P(("vocab", "dp"), None),
    )
    out_specs = (
        P(("vocab", "dp"), None),
        P(("vocab", "dp"), None),
        P(("vocab", "dp"), None),
        P("vocab", None),
    )
    return jax.shard_map(local, mesh=mesh, in_specs=in_specs, out_specs=out_specs, check_vma=False)
```

```python
import jax
import jax.numpy as jnp
from jax import lax
from jax.experimental import pallas as pl
from jax.experimental.pallas import tpu as pltpu
from jax.sharding import PartitionSpec as P

STEP = 8
Z = 16
NX = 4
NY = 4
DP = NX * NY
COLS = 640
NB = 8
UNITS = 48
PARTS = 4
PU = UNITS // PARTS
HALF = ((0, 384), (384, 256))
MESH = pl.DeviceIdType.MESH
F32 = jnp.float32
BF16 = jnp.bfloat16


def update(g, m, mu, nu):
    fn = 0.9 * mu + 0.1 * g
    sn = 0.95 * nu + 0.05 * g * g
    corr1 = 1.0 / (1.0 - 0.9**STEP)
    corr2 = 1.0 / (1.0 - 0.95**STEP)
    mn = m - 0.05 * (fn * corr1 / (jnp.sqrt(sn * corr2) + 1e-08) + 0.1 * m)
    return mn, fn, sn


def kernel(
    hid, logit, mask, slots_in, rows_in, counts, master_in, first_in, second_in,
    grad_o, table,
    slots, master, first, second, hall, masked, outbox, inbox, part0, part1, ring0, ring1, head, ra, r1, q, r2, grad, emb0, emb1, tags_v, ta, tb,
    ag_s, ag_r, sib_s, sib_r, sl_s, sl_r, z_s, z_r,
    ra_s, ra_r, r1_s, r1_r, r2_s, r2_r, e_s, e_r, t1_s, t1_r, t2_s, t2_r, t3_s, t3_r, loc,
):
    d = lax.axis_index("dp")
    v = lax.axis_index("vocab")
    z, c = v // 2, v % 2
    y, x = d // NX, d % NX
    pg, h = d // 2, d % 2
    me = d * 2 + c

    def rc(src, dst, ss, rs, dev):
        return pltpu.make_async_remote_copy(
            src_ref=src, dst_ref=dst, send_sem=ss, recv_sem=rs,
            device_id=dev, device_id_type=MESH)

    up = (d, (v + 2) % 32)
    down = (d, (v + 30) % 32)
    sib = (d, z * 2 + (1 - c))
    zdir = (d, (v + 2 + 28 * c) % 32)

    fetches = [
        pltpu.make_async_copy(src, dst, loc.at[i + 1])
        for i, (src, dst) in enumerate((
            (slots_in, slots), (logit, masked), (master_in, master), (first_in, first), (second_in, second)))
    ]
    for fetch in fetches:
        fetch.start()

    bar = pltpu.get_barrier_semaphore()
    pl.semaphore_signal(bar, inc=1, device_id=up, device_id_type=MESH)
    pl.semaphore_signal(bar, inc=1, device_id=down, device_id_type=MESH)

    def greet(k, carry):
        o = (me + k) % 32
        pl.semaphore_signal(bar, inc=1, device_id=(o // 2, z * 2 + o % 2), device_id_type=MESH)
        return carry

    lax.fori_loop(1, 32, greet, 0)
    pl.semaphore_wait(bar, 33)

    def plane_at(sg, s):
        return (z - s + 16) % 16 if sg == 0 else (z + s) % 16

    def ag(sg, s, half):
        idx = plane_at(sg, s - 1) * 2 + c
        rows = pl.ds(80 * half, 80)
        ref = hall.at[idx, rows]
        src = hid.at[rows] if s == 1 else ref
        return rc(src, ref, ag_s.at[sg, s, half], ag_r.at[sg, s, half], up if sg == 0 else down)

    def ag_arrival(sg, s, half):
        idx = plane_at(sg, s) * 2 + c
        ref = hall.at[idx, pl.ds(80 * half, 80)]
        rc(ref, ref, ag_s.at[sg, s, half], ag_r.at[sg, s, half], up).wait_recv()

    def share(sg, s, half):
        idx = plane_at(sg, s) * 2 + c
        ref = hall.at[idx, pl.ds(80 * half, 80)]
        return rc(ref, ref, sib_s.at[sg, s, half], sib_r.at[sg, s, half], sib)

    def share_arrival(sg, s, half):
        idx = plane_at(sg, s) * 2 + 1 - c
        ref = hall.at[idx, pl.ds(80 * half, 80)]
        rc(ref, ref, sib_s.at[sg, s, half], sib_r.at[sg, s, half], sib).wait_recv()

    own_share = rc(hid, hall.at[v], sib_s.at[0, 0, 0], sib_r.at[0, 0, 0], sib)
    for half in (0, 1):
        ag(0, 1, half).start()
        ag(1, 1, half).start()
    own_share.start()
    own_copy = pltpu.make_async_copy(hid, hall.at[v], loc.at[0])
    own_copy.start()

    part, ring, emb, rowsets = (part0, part1), (ring0, ring1), (emb0, emb1), (ta, tb)

    def row_maps(width):
        r = lax.broadcasted_iota(jnp.int32, (256, width), 0)
        k = lax.broadcasted_iota(jnp.int32, (256, width), 1)
        i = (r // 8) % 8
        to_plane = jnp.where((r // 64) % 2 == 0, z + 24 - i, z + 9 + i) % 16
        return k, r % 8, i, to_plane * 2 + r // 128

    k, e, _, owner = row_maps(192)
    select = jnp.where((e < 6) & (e * 32 + owner == k), 1.0, 0.0).astype(BF16)
    k, e, _, owner = row_maps(32)
    pick = jnp.where((e == 6) & (owner == k), 1.0, 0.0).astype(BF16)
    live = lax.broadcasted_iota(jnp.int32, (6, 32), 0) < counts[...]
    tag = jnp.where(live, rows_in[:, 0, :] + 1, 0).astype(F32)
    tag = jnp.concatenate([tag, jnp.zeros((2, 32), F32)], axis=0).astype(BF16)
    tag = lax.dot_general(pick, tag, (((1,), (1,)), ((), ())), preferred_element_type=F32)
    a = lax.broadcasted_iota(jnp.int32, (8, COLS), 0)
    b = lax.broadcasted_iota(jnp.int32, (8, COLS), 1)
    spread = jnp.where((b % 8 == a) & (b // 16 == me), 1.0, 0.0).astype(BF16)
    tag = jnp.dot(tag.astype(BF16), spread, preferred_element_type=F32)
    k, _, i, _ = row_maps(COLS)
    tags_v[...] = jnp.where((k // 8) % 2 == i % 2, tag, 0.0)

    def slot_copy(g, w, part_of):
        rows = pl.ds(32 * part_of, 32)
        to = (2 * g + w // 2, z * 2 + w % 2)
        return rc(outbox.at[g, w, rows], inbox.at[me, rows],
                  sl_s.at[part_of, g * 4 + w], sl_r.at[part_of, me], to)

    def post(g, part_of):
        rows = pl.ds(32 * part_of, 32)
        for w in range(4):
            mine = (2 * g + w // 2 == d) & (w % 2 == c)

            @pl.when(mine)
            def _():
                pltpu.make_async_copy(
                    outbox.at[g, w, rows], inbox.at[me, rows], sl_r.at[part_of, me]).start()

            @pl.when(jnp.logical_not(mine))
            def _():
                slot_copy(g, w, part_of).start()

    def send_slots(g, carry):
        cols = pl.ds(pl.multiple_of(g * COLS, 128), COLS)
        rows = jnp.dot(select, slots[:, cols], preferred_element_type=F32) + tags_v[...]
        outbox[g] = rows.astype(BF16).reshape(4, 64, COLS)
        post(g, 0)
        return carry

    def send_rest(g, carry):
        post(g, 1)
        return carry

    fetches[0].wait()
    lax.fori_loop(0, 2, send_slots, 0)

    kz = z // 2

    def block_of(n):
        t = (n + 1) // 2
        return (kz + 16 + jnp.where(n % 2 == 1, -t, t)) % NB

    def at_axis(g, xfirst):
        return (y * NX + g, v) if xfirst else (g * NX + x, v)

    def stage0(n, side, xfirst):
        mine = x if xfirst else y
        opp, to = (mine + 2) % 4, (mine + 1 + 2 * side) % 4
        rows = pl.ds(2 * side, 2)
        ref = head.at[n, rows, opp] if xfirst else head.at[n, opp, rows]
        return rc(ref, ra.at[n, side], ra_s.at[n, side], ra_r.at[n, side], at_axis(to, xfirst))

    def stage1(n, side, xfirst):
        to = ((x if xfirst else y) + 1 + 2 * side) % 4
        ref = head.at[n, :, to] if xfirst else head.at[n, to]
        return rc(ref, r1.at[n, side], r1_s.at[n, side], r1_r.at[n, side], at_axis(to, xfirst))

    def stage2(n, g, xfirst):
        if xfirst:
            return rc(q.at[n, g], r2.at[n, y], r2_s.at[n, g], r2_r.at[n, y], (g * NX + x, v))
        return rc(q.at[n, g], r2.at[n, x], r2_s.at[n, g], r2_r.at[n, x], (y * NX + g, v))

    def head_block(n):
        kb = block_of(n)
        rows = hall[pl.ds(4 * kb, 4)].reshape(COLS, 1024)
        val = lax.dot_general(masked[...], rows, (((1,), (1,)), ((), ())), preferred_element_type=F32)
        head[n] = val.reshape(NY, NX, 3, 4, COLS)

    def head_send(n):
        for side in (0, 1):
            stage0(n, side, n % 2 == 0).start()

    def head_add(n):
        xfirst = n % 2 == 0
        mine = x if xfirst else y
        for side in (0, 1):
            ref = ra.at[n, side]
            rc(ref, ref, ra_s.at[n, side], ra_r.at[n, side], up).wait_recv()
            to = (mine + 1 + 2 * side) % 4
            rows = pl.ds(2 * side, 2)
            if xfirst:
                head[n, rows, to] = head[n, rows, to] + ra[n, side]
            else:
                head[n, to, rows] = head[n, to, rows] + ra[n, side]
            stage1(n, side, xfirst).start()

    def head_mid(n):
        xfirst = n % 2 == 0
        for side in (0, 1):
            ref = r1.at[n, side]
            rc(ref, ref, r1_s.at[n, side], r1_r.at[n, side], up).wait_recv()
        own = head[n, :, x] if xfirst else head[n, y]
        q[n] = own + r1[n, 0] + r1[n, 1]
        then = y if xfirst else x
        for o in range(1, 4):
            stage2(n, (then + o) % 4, xfirst).start()

    def head_end(n):
        xfirst = n % 2 == 0
        then = y if xfirst else x
        for o in range(1, 4):
            src = (then + o) % 4
            ref = r2.at[n, src]
            rc(ref, ref, r2_s.at[n, src], r2_r.at[n, src], up).wait_recv()
        grad[block_of(n)] = (
            q[n, then] + r2[n, (then + 1) % 4] + r2[n, (then + 2) % 4] + r2[n, (then + 3) % 4]
        )

    def ag_step(s):
        for half in (0, 1):
            for sg in (0, 1):
                if s == 8 and half != sg:
                    continue
                ag_arrival(sg, s, half)
                if s < 7 or (s == 7 and half == sg):
                    ag(sg, s + 1, half).start()
                share(sg, s, half).start()

    def shares_of(s):
        for half in (0, 1):
            for sg in (0, 1):
                if s == 8 and half != sg:
                    continue
                share_arrival(sg, s, half)

    def embed_parts(part_of):
        def arrived(s, carry):
            ref = inbox.at[s, pl.ds(32 * part_of, 32)]
            rc(ref, ref, sl_s.at[part_of, s], sl_r.at[part_of, s], up).wait_recv()
            return carry

        lax.fori_loop(0, 32, arrived, 0)

        def pair(p, carry):
            rows = inbox[:, pl.ds(pl.multiple_of(16 * p, 16), 16), :]
            tags = rows[:, :, :512].astype(F32)
            sub = lax.broadcasted_iota(jnp.int32, (32, 16, 512), 1)
            tags = jnp.where(sub % 8 == 6, tags, 0.0)
            tags = jnp.sum(jnp.sum(tags, axis=0), axis=0, keepdims=True)
            lane = lax.broadcasted_iota(jnp.int32, (1, 512), 1)
            shift = jnp.where((lane // 8) % 2 == 1, 192.0, 0.0)
            tags = jnp.where(tags > 0.5, tags + shift, 0.0)
            row = lax.broadcasted_iota(jnp.int32, (384, 512), 0).astype(F32) + 1.0
            hot = jnp.where(row == tags, 1.0, 0.0).astype(BF16)
            val = jnp.dot(hot, rows.reshape(512, COLS), preferred_element_type=F32)
            for a, (off, n) in enumerate(HALF):
                part[a][pl.ds(2 * p, 2)] = val[:, off:off + n].reshape(2, UNITS, 4, n)
            return carry

        lax.fori_loop(2 * part_of, 2 * part_of + 2, pair, 0)

    def z_copy(s, src, p, a):
        rows = pl.ds(p * PU, PU)
        return rc(src.at[rows], ring[a].at[s, rows], z_s.at[a, s, p], z_r.at[a, s, p], zdir)

    def z_arrival(s, p, a):
        ref = ring[a].at[s, pl.ds(p * PU, PU)]
        rc(ref, ref, z_s.at[a, s, p], z_r.at[a, s, p], zdir).wait_recv()

    def z_step(s, a):
        for p in range(PARTS):
            if s == 0:
                z_copy(0, part[a].at[0], p, a).start()
                continue
            z_arrival(s - 1, p, a)
            rows = pl.ds(p * PU, PU)
            ring[a][s - 1, rows] = ring[a][s - 1, rows] + part[a][s, rows]
            if s < 7:
                z_copy(s, ring[a].at[s - 1], p, a).start()
            else:

                @pl.when(c == 0)
                def _():
                    z_copy(s, ring[a].at[s - 1], p, a).start()

    fin = 7 - c

    def e_refs(t, a):
        return ring[a].at[fin, pl.ds(3 * t, 3)], emb[a].at[c, pg]

    def e_copy(t, a):
        src, dst = e_refs(t, a)
        return rc(src, dst, e_s.at[a, t], e_r.at[a, c, pg], (t, z * 2 + h))

    def finish(a):
        for p in range(PARTS):

            @pl.when(c == 0)
            def _():
                z_arrival(7, p, a)

            for t in range(4 * p, 4 * p + 4):
                mine = (t == d) & (h == c)

                @pl.when(mine)
                def _():
                    src, dst = e_refs(t, a)
                    pltpu.make_async_copy(src, dst, e_r.at[a, c, pg]).start()

                @pl.when(jnp.logical_not(mine))
                def _():
                    e_copy(t, a).start()

    def adam(a):
        if a == 0:
            for fetch in fetches[2:]:
                fetch.wait()
        off, n = HALF[a]
        for b in range(NB):
            cut = pl.ds(off, n)
            for w in (0, 1):
                ref = emb[a].at[w, b]
                rc(ref, ref, e_s.at[a, b], e_r.at[a, w, b], up).wait_recv()
            g = grad[b, :, :, cut] + emb[a][0, b] + emb[a][1, b]
            g = jnp.concatenate([g[0], g[1], g[2]], axis=0)
            cols = pl.ds(b * COLS + off, n)
            mn, _, _ = update(g, master[:, cols], first[:, cols], second[:, cols])
            grad_o[:, cols] = g
            mn = mn.astype(BF16)
            for u in range(3):
                rowsets[a][b // 4, y, x, u, :, pl.ds((b % 4) * n, n)] = mn[4 * u:4 * u + 4]

    firsts = (x, y)
    seconds = (y, x)

    def group(a, w, g):
        return rowsets[a].at[w, g] if w == 0 else rowsets[a].at[w, :, g]

    def t1(a, w, g):
        ref = rowsets[a].at[w, y, x]
        to = (y * NX + g, v) if w == 0 else (g * NX + x, v)
        return rc(ref, ref, t1_s.at[a, w, g], t1_r.at[a, w, firsts[w]], to)

    def t2(a, w, side):
        ref = group(a, w, seconds[w])
        to = at_axis((seconds[w] + 1 + 2 * side) % 4, w == 1)
        return rc(ref, ref, t2_s.at[a, w, side], t2_r.at[a, w, side], to)

    def t3(a, w, side):
        g = (seconds[w] + 3 + 2 * side) % 4
        ref = group(a, w, g).at[pl.ds(2 * side, 2)]
        to = at_axis((seconds[w] + 1 + 2 * side) % 4, w == 1)
        return rc(ref, ref, t3_s.at[a, w, side], t3_r.at[a, w, side], to)

    def spread_rows(a):
        for o in range(1, 4):
            for w in (0, 1):
                t1(a, w, (firsts[w] + o) % 4).start()

    def spread_groups(a):
        for w in (0, 1):
            for o in range(1, 4):
                g = (firsts[w] + o) % 4
                ref = rowsets[a].at[w, y, g] if w == 0 else rowsets[a].at[w, g, x]
                rc(ref, ref, t1_s.at[a, w, g], t1_r.at[a, w, g], up).wait_recv()
            for side in (0, 1):
                t2(a, w, side).start()

    def pass_groups(a):
        for w in (0, 1):
            for side in (0, 1):
                ref = group(a, w, (seconds[w] + 3 + 2 * side) % 4)
                rc(ref, ref, t2_s.at[a, w, side], t2_r.at[a, w, side], up).wait_recv()
                t3(a, w, side).start()

    def gathered(a):
        for w in (0, 1):
            for side in (0, 1):
                ref = group(a, w, (seconds[w] + 2) % 4).at[pl.ds(2 * side, 2)]
                rc(ref, ref, t3_s.at[a, w, side], t3_r.at[a, w, side], up).wait_recv()

    def write_table(a):
        off, n = HALF[a]
        for w in (0, 1):
            for b in range(4):
                for m in range(12):
                    units = [4 * m + i for i in range(4)]
                    cut = pl.ds(b * n, n)
                    rows = [rowsets[a][w, t // 12, (t // 3) % 4, t % 3, :, cut] for t in units]
                    table[pl.ds(16 * m, 16), pl.ds((4 * w + b) * COLS + off, n)] = jnp.concatenate(rows, axis=0)

    own_copy.wait()
    ag_step(1)
    lax.fori_loop(2, 5, send_slots, 0)
    ag_step(2)
    lax.fori_loop(5, 8, send_slots, 0)
    own_idx = v + 1 - 2 * c
    rc(hid, hall.at[own_idx], sib_s.at[0, 0, 0], sib_r.at[0, 0, 0], sib).wait_recv()
    fetches[1].wait()
    masked[...] = masked[...] * mask[...].astype(BF16)
    ag_step(3)
    lax.fori_loop(0, 8, send_rest, 0)
    shares_of(1)
    head_block(0)
    shares_of(2)
    shares_of(3)
    ag_step(4)
    head_block(1)
    head_block(2)
    ag_step(5)
    shares_of(4)
    shares_of(5)
    head_block(3)
    ag_step(6)
    head_block(4)
    ag_step(7)
    embed_parts(0)
    z_step(0, 0)
    for n in range(5):
        head_send(n)
    shares_of(6)
    shares_of(7)
    head_block(5)
    head_block(6)
    head_send(5)
    head_send(6)
    ag_step(8)
    z_step(1, 0)
    shares_of(8)
    head_block(7)
    head_send(7)
    head_add(0)
    head_add(1)
    z_step(2, 0)
    head_add(2)
    head_add(3)
    head_add(4)
    z_step(3, 0)
    embed_parts(1)
    z_step(4, 0)
    head_mid(0)
    head_mid(1)
    head_add(5)
    head_add(6)
    head_add(7)
    z_step(5, 0)
    head_mid(2)
    head_mid(3)
    head_mid(4)
    z_step(6, 0)
    z_step(0, 1)
    head_mid(5)
    head_mid(6)
    head_mid(7)
    head_end(0)
    head_end(1)
    z_step(7, 0)
    z_step(1, 1)
    finish(0)
    head_end(2)
    head_end(3)
    z_step(2, 1)
    head_end(4)
    head_end(5)
    z_step(3, 1)
    head_end(6)
    head_end(7)
    z_step(4, 1)
    adam(0)
    spread_rows(0)
    z_step(5, 1)
    z_step(6, 1)
    spread_groups(0)
    z_step(7, 1)
    finish(1)
    pass_groups(0)
    gathered(0)
    write_table(0)
    adam(1)
    spread_rows(1)
    spread_groups(1)
    pass_groups(1)
    gathered(1)
    write_table(1)

    own_share.wait_send()
    for s in range(1, 9):
        for half in (0, 1):
            for sg in (0, 1):
                if s == 8 and half != sg:
                    continue
                ag(sg, s, half).wait_send()
                share(sg, s, half).wait_send()

    def slots_left(g, carry):
        for w in range(4):

            @pl.when(jnp.logical_not((2 * g + w // 2 == d) & (w % 2 == c)))
            def _():
                slot_copy(g, w, 0).wait_send()
                slot_copy(g, w, 1).wait_send()
        return carry

    lax.fori_loop(0, NB, slots_left, 0)
    for n in range(NB):
        xfirst = n % 2 == 0
        for side in (0, 1):
            stage0(n, side, xfirst).wait_send()
            stage1(n, side, xfirst).wait_send()
        for o in range(1, 4):
            stage2(n, ((y if xfirst else x) + o) % 4, xfirst).wait_send()
    for a in (0, 1):
        for s in range(8):
            for p in range(PARTS):
                src = part[a].at[0] if s == 0 else ring[a].at[s - 1]
                if s < 7:
                    z_copy(s, src, p, a).wait_send()
                else:

                    @pl.when(c == 0)
                    def _():
                        z_copy(s, src, p, a).wait_send()
        for t in range(DP):

            @pl.when(jnp.logical_not((t == d) & (h == c)))
            def _():
                e_copy(t, a).wait_send()
        for w in (0, 1):
            for o in range(1, 4):
                t1(a, w, (firsts[w] + o) % 4).wait_send()
            for side in (0, 1):
                t2(a, w, side).wait_send()
                t3(a, w, side).wait_send()


def local(hidden, logit_grad, predict_mask, slot_grads, slot_rows, slot_counts, master, first, second):
    slots = slot_grads[0].transpose(1, 0, 2).reshape(192, 5120)
    rows_in = slot_rows.transpose(2, 0, 1)
    vm = pl.BlockSpec(memory_space=pltpu.VMEM)
    hbm = pl.BlockSpec(memory_space=pl.ANY)
    dma = pltpu.SemaphoreType.DMA
    grad, table = pl.pallas_call(
        kernel,
        out_shape=(
            jax.ShapeDtypeStruct((12, 5120), F32),
            jax.ShapeDtypeStruct((192, 5120), BF16),
        ),
        in_specs=[hbm, hbm, vm, hbm, vm, vm, hbm, hbm, hbm],
        out_specs=(vm,) * 2,
        scratch_shapes=[
            pltpu.VMEM((192, 5120), BF16),
            pltpu.VMEM((12, 5120), F32),
            pltpu.VMEM((12, 5120), F32),
            pltpu.VMEM((12, 5120), F32),
            pltpu.VMEM((32, 160, 1024), BF16),
            pltpu.VMEM((192, 1024), BF16),
            pltpu.VMEM((NB, 4, 64, COLS), BF16),
            pltpu.VMEM((32, 64, COLS), BF16),
            pltpu.VMEM((8, UNITS, 4, HALF[0][1]), F32),
            pltpu.VMEM((8, UNITS, 4, HALF[1][1]), F32),
            pltpu.VMEM((8, UNITS, 4, HALF[0][1]), F32),
            pltpu.VMEM((8, UNITS, 4, HALF[1][1]), F32),
            pltpu.VMEM((NB, NY, NX, 3, 4, COLS), F32),
            pltpu.VMEM((NB, 2, 2, 3, 4, COLS), F32),
            pltpu.VMEM((NB, 2, 4, 3, 4, COLS), F32),
            pltpu.VMEM((NB, 4, 3, 4, COLS), F32),
            pltpu.VMEM((NB, 4, 3, 4, COLS), F32),
            pltpu.VMEM((NB, 3, 4, COLS), F32),
            pltpu.VMEM((2, NB, 3, 4, HALF[0][1]), F32),
            pltpu.VMEM((2, NB, 3, 4, HALF[1][1]), F32),
            pltpu.VMEM((256, COLS), F32),
            pltpu.VMEM((2, NY, NX, 3, 4, 4 * HALF[0][1]), BF16),
            pltpu.VMEM((2, NY, NX, 3, 4, 4 * HALF[1][1]), BF16),
            dma((2, 9, 2)), dma((2, 9, 2)), dma((2, 9, 2)), dma((2, 9, 2)),
            dma((2, 32)), dma((2, 32)), dma((2, 8, PARTS)), dma((2, 8, PARTS)),
            dma((NB, 2)), dma((NB, 2)), dma((NB, 2)), dma((NB, 2)), dma((NB, 4)), dma((NB, 4)),
            dma((2, DP)), dma((2, 2, NB)),
            dma((2, 2, 4)), dma((2, 2, 4)), dma((2, 2, 2)), dma((2, 2, 2)), dma((2, 2, 2)), dma((2, 2, 2)),
            dma((6,)),
        ],
        compiler_params=pltpu.CompilerParams(
            collective_id=0, has_side_effects=True, vmem_limit_bytes=60 * 1024 * 1024),
    )(hidden.T, logit_grad.T, predict_mask[None, :], slots, rows_in, slot_counts, master, first, second)
    return (*update(grad, master, first, second), table)


def solution(mesh):
    in_specs = (
        P("dp", "vocab"),
        P("dp", "vocab"),
        P("dp"),
        P(("dp", "vocab"), None, None, None),
        P(("dp", "vocab"), None, None),
        P(("dp", "vocab"), None),
        P(("vocab", "dp"), None),
        P(("vocab", "dp"), None),
        P(("vocab", "dp"), None),
    )
    out_specs = (
        P(("vocab", "dp"), None),
        P(("vocab", "dp"), None),
        P(("vocab", "dp"), None),
        P("vocab", None),
    )
    return jax.shard_map(local, mesh=mesh, in_specs=in_specs, out_specs=out_specs, check_vma=False)
```

```python
import jax
import jax.numpy as jnp
from jax import lax
from jax.experimental import pallas as pl
from jax.experimental.pallas import tpu as pltpu
from jax.sharding import PartitionSpec as P

STEP = 8
Z = 16
NX = 4
NY = 4
DP = NX * NY
COLS = 640
NB = 8
UNITS = 48
PARTS = 4
PU = UNITS // PARTS
HALF = ((0, 384), (384, 256))
MESH = pl.DeviceIdType.MESH
F32 = jnp.float32
BF16 = jnp.bfloat16


def update(g, m, mu, nu):
    fn = 0.9 * mu + 0.1 * g
    sn = 0.95 * nu + 0.05 * g * g
    corr1 = 1.0 / (1.0 - 0.9**STEP)
    corr2 = 1.0 / (1.0 - 0.95**STEP)
    mn = m - 0.05 * (fn * corr1 / (jnp.sqrt(sn * corr2) + 1e-08) + 0.1 * m)
    return mn, fn, sn


def kernel(
    hid, logit, mask, slots_in, rows_in, counts, master_in, first_in, second_in,
    grad_o, table,
    slots, master, first, second, hall, masked, outbox, inbox, part0, part1, ring0, ring1, head, ra, r1, q, r2, grad, emb0, emb1, tags_v, ta, tb,
    ag_s, ag_r, sib_s, sib_r, sl_s, sl_r, z_s, z_r,
    ra_s, ra_r, r1_s, r1_r, r2_s, r2_r, e_s, e_r, t1_s, t1_r, t2_s, t2_r, t3_s, t3_r, loc,
):
    d = lax.axis_index("dp")
    v = lax.axis_index("vocab")
    z, c = v // 2, v % 2
    y, x = d // NX, d % NX
    pg, h = d // 2, d % 2
    me = d * 2 + c

    def rc(src, dst, ss, rs, dev):
        return pltpu.make_async_remote_copy(
            src_ref=src, dst_ref=dst, send_sem=ss, recv_sem=rs,
            device_id=dev, device_id_type=MESH)

    up = (d, (v + 2) % 32)
    down = (d, (v + 30) % 32)
    sib = (d, z * 2 + (1 - c))
    zdir = (d, (v + 2 + 28 * c) % 32)

    fetches = [
        pltpu.make_async_copy(src, dst, loc.at[i + 1])
        for i, (src, dst) in enumerate((
            (slots_in, slots), (logit, masked), (master_in, master), (first_in, first), (second_in, second)))
    ]
    for fetch in fetches:
        fetch.start()

    bar = pltpu.get_barrier_semaphore()
    pl.semaphore_signal(bar, inc=1, device_id=up, device_id_type=MESH)
    pl.semaphore_signal(bar, inc=1, device_id=down, device_id_type=MESH)

    def greet(k, carry):
        o = (me + k) % 32
        pl.semaphore_signal(bar, inc=1, device_id=(o // 2, z * 2 + o % 2), device_id_type=MESH)
        return carry

    lax.fori_loop(1, 32, greet, 0)
    pl.semaphore_wait(bar, 33)

    def plane_at(sg, s):
        return (z - s + 16) % 16 if sg == 0 else (z + s) % 16

    def ag(sg, s, half):
        idx = plane_at(sg, s - 1) * 2 + c
        rows = pl.ds(80 * half, 80)
        ref = hall.at[idx, rows]
        src = hid.at[rows] if s == 1 else ref
        return rc(src, ref, ag_s.at[sg, s, half], ag_r.at[sg, s, half], up if sg == 0 else down)

    def ag_arrival(sg, s, half):
        idx = plane_at(sg, s) * 2 + c
        ref = hall.at[idx, pl.ds(80 * half, 80)]
        rc(ref, ref, ag_s.at[sg, s, half], ag_r.at[sg, s, half], up).wait_recv()

    def share(sg, s, half):
        idx = plane_at(sg, s) * 2 + c
        ref = hall.at[idx, pl.ds(80 * half, 80)]
        return rc(ref, ref, sib_s.at[sg, s, half], sib_r.at[sg, s, half], sib)

    def share_arrival(sg, s, half):
        idx = plane_at(sg, s) * 2 + 1 - c
        ref = hall.at[idx, pl.ds(80 * half, 80)]
        rc(ref, ref, sib_s.at[sg, s, half], sib_r.at[sg, s, half], sib).wait_recv()

    own_share = rc(hid, hall.at[v], sib_s.at[0, 0, 0], sib_r.at[0, 0, 0], sib)
    for half in (0, 1):
        ag(0, 1, half).start()
        ag(1, 1, half).start()
    own_share.start()
    own_copy = pltpu.make_async_copy(hid, hall.at[v], loc.at[0])
    own_copy.start()

    part, ring, emb, rowsets = (part0, part1), (ring0, ring1), (emb0, emb1), (ta, tb)

    def row_maps(width):
        r = lax.broadcasted_iota(jnp.int32, (256, width), 0)
        k = lax.broadcasted_iota(jnp.int32, (256, width), 1)
        i = (r // 8) % 8
        to_plane = jnp.where((r // 64) % 2 == 0, z + 24 - i, z + 9 + i) % 16
        return k, r % 8, i, to_plane * 2 + r // 128

    k, e, _, owner = row_maps(192)
    select = jnp.where((e < 6) & (e * 32 + owner == k), 1.0, 0.0).astype(BF16)
    k, e, _, owner = row_maps(32)
    pick = jnp.where((e == 6) & (owner == k), 1.0, 0.0).astype(BF16)
    live = lax.broadcasted_iota(jnp.int32, (6, 32), 0) < counts[...]
    tag = jnp.where(live, rows_in[:, 0, :] + 1, 0).astype(F32)
    tag = jnp.concatenate([tag, jnp.zeros((2, 32), F32)], axis=0).astype(BF16)
    tag = lax.dot_general(pick, tag, (((1,), (1,)), ((), ())), preferred_element_type=F32)
    a = lax.broadcasted_iota(jnp.int32, (8, COLS), 0)
    b = lax.broadcasted_iota(jnp.int32, (8, COLS), 1)
    spread = jnp.where((b % 8 == a) & (b // 16 == me), 1.0, 0.0).astype(BF16)
    tag = jnp.dot(tag.astype(BF16), spread, preferred_element_type=F32)
    k, _, i, _ = row_maps(COLS)
    tags_v[...] = jnp.where((k // 8) % 2 == i % 2, tag, 0.0)

    def slot_copy(g, w, part_of):
        rows = pl.ds(32 * part_of, 32)
        to = (2 * g + w // 2, z * 2 + w % 2)
        return rc(outbox.at[g, w, rows], inbox.at[me, rows],
                  sl_s.at[part_of, g * 4 + w], sl_r.at[part_of, me], to)

    def post(g, part_of):
        rows = pl.ds(32 * part_of, 32)
        for w in range(4):
            mine = (2 * g + w // 2 == d) & (w % 2 == c)

            @pl.when(mine)
            def _():
                pltpu.make_async_copy(
                    outbox.at[g, w, rows], inbox.at[me, rows], sl_r.at[part_of, me]).start()

            @pl.when(jnp.logical_not(mine))
            def _():
                slot_copy(g, w, part_of).start()

    def send_slots(g, carry):
        cols = pl.ds(pl.multiple_of(g * COLS, 128), COLS)
        rows = jnp.dot(select, slots[:, cols], preferred_element_type=F32) + tags_v[...]
        outbox[g] = rows.astype(BF16).reshape(4, 64, COLS)
        post(g, 0)
        return carry

    def send_rest(g, carry):
        post(g, 1)
        return carry

    fetches[0].wait()
    lax.fori_loop(0, 2, send_slots, 0)

    kz = z // 2

    def block_of(n):
        t = (n + 1) // 2
        return (kz + 16 + jnp.where(n % 2 == 1, -t, t)) % NB

    def at_axis(g, xfirst):
        return (y * NX + g, v) if xfirst else (g * NX + x, v)

    def stage0(n, side, xfirst):
        mine = x if xfirst else y
        opp, to = (mine + 2) % 4, (mine + 1 + 2 * side) % 4
        rows = pl.ds(2 * side, 2)
        ref = head.at[n, rows, opp] if xfirst else head.at[n, opp, rows]
        return rc(ref, ra.at[n, side], ra_s.at[n, side], ra_r.at[n, side], at_axis(to, xfirst))

    def stage1(n, side, xfirst):
        to = ((x if xfirst else y) + 1 + 2 * side) % 4
        ref = head.at[n, :, to] if xfirst else head.at[n, to]
        return rc(ref, r1.at[n, side], r1_s.at[n, side], r1_r.at[n, side], at_axis(to, xfirst))

    def stage2(n, g, xfirst):
        if xfirst:
            return rc(q.at[n, g], r2.at[n, y], r2_s.at[n, g], r2_r.at[n, y], (g * NX + x, v))
        return rc(q.at[n, g], r2.at[n, x], r2_s.at[n, g], r2_r.at[n, x], (y * NX + g, v))

    def head_block(n):
        kb = block_of(n)
        rows = hall[pl.ds(4 * kb, 4)].reshape(COLS, 1024)
        val = lax.dot_general(masked[...], rows, (((1,), (1,)), ((), ())), preferred_element_type=F32)
        head[n] = val.reshape(NY, NX, 3, 4, COLS)

    def head_send(n):
        for side in (0, 1):
            stage0(n, side, n % 2 == 0).start()

    def head_add(n):
        xfirst = n % 2 == 0
        mine = x if xfirst else y
        for side in (0, 1):
            ref = ra.at[n, side]
            rc(ref, ref, ra_s.at[n, side], ra_r.at[n, side], up).wait_recv()
            to = (mine + 1 + 2 * side) % 4
            rows = pl.ds(2 * side, 2)
            if xfirst:
                head[n, rows, to] = head[n, rows, to] + ra[n, side]
            else:
                head[n, to, rows] = head[n, to, rows] + ra[n, side]
            stage1(n, side, xfirst).start()

    def head_mid(n):
        xfirst = n % 2 == 0
        for side in (0, 1):
            ref = r1.at[n, side]
            rc(ref, ref, r1_s.at[n, side], r1_r.at[n, side], up).wait_recv()
        own = head[n, :, x] if xfirst else head[n, y]
        q[n] = own + r1[n, 0] + r1[n, 1]
        then = y if xfirst else x
        for o in range(1, 4):
            stage2(n, (then + o) % 4, xfirst).start()

    def head_end(n):
        xfirst = n % 2 == 0
        then = y if xfirst else x
        for o in range(1, 4):
            src = (then + o) % 4
            ref = r2.at[n, src]
            rc(ref, ref, r2_s.at[n, src], r2_r.at[n, src], up).wait_recv()
        grad[block_of(n)] = (
            q[n, then] + r2[n, (then + 1) % 4] + r2[n, (then + 2) % 4] + r2[n, (then + 3) % 4]
        )

    def ag_step(s):
        for half in (0, 1):
            for sg in (0, 1):
                if s == 8 and half != sg:
                    continue
                ag_arrival(sg, s, half)
                if s < 7 or (s == 7 and half == sg):
                    ag(sg, s + 1, half).start()
                share(sg, s, half).start()

    def shares_of(s):
        for half in (0, 1):
            for sg in (0, 1):
                if s == 8 and half != sg:
                    continue
                share_arrival(sg, s, half)

    def embed_parts(part_of):
        def arrived(s, carry):
            ref = inbox.at[s, pl.ds(32 * part_of, 32)]
            rc(ref, ref, sl_s.at[part_of, s], sl_r.at[part_of, s], up).wait_recv()
            return carry

        lax.fori_loop(0, 32, arrived, 0)

        def pair(p, carry):
            rows = inbox[:, pl.ds(pl.multiple_of(16 * p, 16), 16), :]
            tags = rows[:, :, :512].astype(F32)
            sub = lax.broadcasted_iota(jnp.int32, (32, 16, 512), 1)
            tags = jnp.where(sub % 8 == 6, tags, 0.0)
            tags = jnp.sum(jnp.sum(tags, axis=0), axis=0, keepdims=True)
            lane = lax.broadcasted_iota(jnp.int32, (1, 512), 1)
            shift = jnp.where((lane // 8) % 2 == 1, 192.0, 0.0)
            tags = jnp.where(tags > 0.5, tags + shift, 0.0)
            row = lax.broadcasted_iota(jnp.int32, (384, 512), 0).astype(F32) + 1.0
            hot = jnp.where(row == tags, 1.0, 0.0).astype(BF16)
            val = jnp.dot(hot, rows.reshape(512, COLS), preferred_element_type=F32)
            for a, (off, n) in enumerate(HALF):
                part[a][pl.ds(2 * p, 2)] = val[:, off:off + n].reshape(2, UNITS, 4, n)
            return carry

        lax.fori_loop(2 * part_of, 2 * part_of + 2, pair, 0)

    def z_copy(s, src, p, a):
        rows = pl.ds(p * PU, PU)
        return rc(src.at[rows], ring[a].at[s, rows], z_s.at[a, s, p], z_r.at[a, s, p], zdir)

    def z_arrival(s, p, a):
        ref = ring[a].at[s, pl.ds(p * PU, PU)]
        rc(ref, ref, z_s.at[a, s, p], z_r.at[a, s, p], zdir).wait_recv()

    def z_step(s, a):
        for p in range(PARTS):
            if s == 0:
                z_copy(0, part[a].at[0], p, a).start()
                continue
            z_arrival(s - 1, p, a)
            rows = pl.ds(p * PU, PU)
            ring[a][s - 1, rows] = ring[a][s - 1, rows] + part[a][s, rows]
            if s < 7:
                z_copy(s, ring[a].at[s - 1], p, a).start()
            else:

                @pl.when(c == 0)
                def _():
                    z_copy(s, ring[a].at[s - 1], p, a).start()

    fin = 7 - c

    def e_refs(t, a):
        return ring[a].at[fin, pl.ds(3 * t, 3)], emb[a].at[c, pg]

    def e_copy(t, a):
        src, dst = e_refs(t, a)
        return rc(src, dst, e_s.at[a, t], e_r.at[a, c, pg], (t, z * 2 + h))

    def finish(a):
        for p in range(PARTS):

            @pl.when(c == 0)
            def _():
                z_arrival(7, p, a)

            for t in range(4 * p, 4 * p + 4):
                mine = (t == d) & (h == c)

                @pl.when(mine)
                def _():
                    src, dst = e_refs(t, a)
                    pltpu.make_async_copy(src, dst, e_r.at[a, c, pg]).start()

                @pl.when(jnp.logical_not(mine))
                def _():
                    e_copy(t, a).start()

    def adam(a):
        if a == 0:
            for fetch in fetches[2:]:
                fetch.wait()
        off, n = HALF[a]
        for b in range(NB):
            cut = pl.ds(off, n)
            for w in (0, 1):
                ref = emb[a].at[w, b]
                rc(ref, ref, e_s.at[a, b], e_r.at[a, w, b], up).wait_recv()
            g = grad[b, :, :, cut] + emb[a][0, b] + emb[a][1, b]
            g = jnp.concatenate([g[0], g[1], g[2]], axis=0)
            cols = pl.ds(b * COLS + off, n)
            mn, _, _ = update(g, master[:, cols], first[:, cols], second[:, cols])
            grad_o[:, cols] = g
            mn = mn.astype(BF16)
            for u in range(3):
                rowsets[a][b // 4, y, x, u, :, pl.ds((b % 4) * n, n)] = mn[4 * u:4 * u + 4]

    firsts = (x, y)
    seconds = (y, x)

    def group(a, w, g):
        return rowsets[a].at[w, g] if w == 0 else rowsets[a].at[w, :, g]

    def t1(a, w, g):
        ref = rowsets[a].at[w, y, x]
        to = (y * NX + g, v) if w == 0 else (g * NX + x, v)
        return rc(ref, ref, t1_s.at[a, w, g], t1_r.at[a, w, firsts[w]], to)

    def t2(a, w, side):
        ref = group(a, w, seconds[w])
        to = at_axis((seconds[w] + 1 + 2 * side) % 4, w == 1)
        return rc(ref, ref, t2_s.at[a, w, side], t2_r.at[a, w, side], to)

    def t3(a, w, side):
        g = (seconds[w] + 3 + 2 * side) % 4
        ref = group(a, w, g).at[pl.ds(2 * side, 2)]
        to = at_axis((seconds[w] + 1 + 2 * side) % 4, w == 1)
        return rc(ref, ref, t3_s.at[a, w, side], t3_r.at[a, w, side], to)

    def spread_rows(a):
        for o in range(1, 4):
            for w in (0, 1):
                t1(a, w, (firsts[w] + o) % 4).start()

    def spread_groups(a):
        for w in (0, 1):
            for o in range(1, 4):
                g = (firsts[w] + o) % 4
                ref = rowsets[a].at[w, y, g] if w == 0 else rowsets[a].at[w, g, x]
                rc(ref, ref, t1_s.at[a, w, g], t1_r.at[a, w, g], up).wait_recv()
            for side in (0, 1):
                t2(a, w, side).start()

    def pass_groups(a):
        for w in (0, 1):
            for side in (0, 1):
                ref = group(a, w, (seconds[w] + 3 + 2 * side) % 4)
                rc(ref, ref, t2_s.at[a, w, side], t2_r.at[a, w, side], up).wait_recv()
                t3(a, w, side).start()

    def gathered(a):
        for w in (0, 1):
            for side in (0, 1):
                ref = group(a, w, (seconds[w] + 2) % 4).at[pl.ds(2 * side, 2)]
                rc(ref, ref, t3_s.at[a, w, side], t3_r.at[a, w, side], up).wait_recv()

    def write_table(a):
        off, n = HALF[a]
        for w in (0, 1):
            for b in range(4):
                for m in range(12):
                    units = [4 * m + i for i in range(4)]
                    cut = pl.ds(b * n, n)
                    rows = [rowsets[a][w, t // 12, (t // 3) % 4, t % 3, :, cut] for t in units]
                    table[pl.ds(16 * m, 16), pl.ds((4 * w + b) * COLS + off, n)] = jnp.concatenate(rows, axis=0)

    def hidden_left():
        own_share.wait_send()
        for s in range(1, 9):
            for half in (0, 1):
                for sg in (0, 1):
                    if s == 8 and half != sg:
                        continue
                    ag(sg, s, half).wait_send()
                    share(sg, s, half).wait_send()

    def slots_left(g, carry):
        for w in range(4):

            @pl.when(jnp.logical_not((2 * g + w // 2 == d) & (w % 2 == c)))
            def _():
                slot_copy(g, w, 0).wait_send()
                slot_copy(g, w, 1).wait_send()
        return carry

    def head_left():
        for n in range(NB):
            xfirst = n % 2 == 0
            for side in (0, 1):
                stage0(n, side, xfirst).wait_send()
                stage1(n, side, xfirst).wait_send()
            for o in range(1, 4):
                stage2(n, ((y if xfirst else x) + o) % 4, xfirst).wait_send()

    def ring_left(a):
        for s in range(8):
            for p in range(PARTS):
                src = part[a].at[0] if s == 0 else ring[a].at[s - 1]
                if s < 7:
                    z_copy(s, src, p, a).wait_send()
                else:

                    @pl.when(c == 0)
                    def _():
                        z_copy(s, src, p, a).wait_send()

    def rows_left(a):
        for t in range(DP):

            @pl.when(jnp.logical_not((t == d) & (h == c)))
            def _():
                e_copy(t, a).wait_send()

    def table_left(a):
        for w in (0, 1):
            for o in range(1, 4):
                t1(a, w, (firsts[w] + o) % 4).wait_send()
            for side in (0, 1):
                t2(a, w, side).wait_send()
                t3(a, w, side).wait_send()

    own_copy.wait()
    ag_step(1)
    lax.fori_loop(2, 5, send_slots, 0)
    ag_step(2)
    lax.fori_loop(5, 8, send_slots, 0)
    own_idx = v + 1 - 2 * c
    rc(hid, hall.at[own_idx], sib_s.at[0, 0, 0], sib_r.at[0, 0, 0], sib).wait_recv()
    fetches[1].wait()
    masked[...] = masked[...] * mask[...].astype(BF16)
    ag_step(3)
    lax.fori_loop(0, 8, send_rest, 0)
    shares_of(1)
    head_block(0)
    shares_of(2)
    shares_of(3)
    ag_step(4)
    head_block(1)
    head_block(2)
    ag_step(5)
    shares_of(4)
    shares_of(5)
    head_block(3)
    for n in range(3):
        head_send(n)
    ag_step(6)
    head_block(4)
    head_send(3)
    head_send(4)
    ag_step(7)
    embed_parts(0)
    z_step(0, 0)
    shares_of(6)
    shares_of(7)
    head_block(5)
    head_block(6)
    head_send(5)
    head_send(6)
    ag_step(8)
    z_step(1, 0)
    shares_of(8)
    head_block(7)
    head_send(7)
    head_add(0)
    head_add(1)
    z_step(2, 0)
    head_add(2)
    head_add(3)
    head_add(4)
    z_step(3, 0)
    embed_parts(1)
    z_step(4, 0)
    head_mid(0)
    head_mid(1)
    head_add(5)
    head_add(6)
    head_add(7)
    z_step(5, 0)
    head_mid(2)
    head_mid(3)
    head_mid(4)
    z_step(6, 0)
    z_step(0, 1)
    head_mid(5)
    head_mid(6)
    head_mid(7)
    head_end(0)
    head_end(1)
    z_step(7, 0)
    z_step(1, 1)
    finish(0)
    hidden_left()
    head_end(2)
    head_end(3)
    z_step(2, 1)
    head_end(4)
    head_end(5)
    z_step(3, 1)
    head_end(6)
    head_end(7)
    lax.fori_loop(0, NB, slots_left, 0)
    z_step(4, 1)
    adam(0)
    spread_rows(0)
    z_step(5, 1)
    z_step(6, 1)
    spread_groups(0)
    z_step(7, 1)
    finish(1)
    pass_groups(0)
    ring_left(0)
    head_left()
    adam(1)
    spread_rows(1)
    gathered(0)
    write_table(0)
    rows_left(0)
    spread_groups(1)
    ring_left(1)
    pass_groups(1)
    rows_left(1)
    table_left(0)
    gathered(1)
    write_table(1)
    table_left(1)


def local(hidden, logit_grad, predict_mask, slot_grads, slot_rows, slot_counts, master, first, second):
    slots = slot_grads[0].transpose(1, 0, 2).reshape(192, 5120)
    rows_in = slot_rows.transpose(2, 0, 1)
    vm = pl.BlockSpec(memory_space=pltpu.VMEM)
    hbm = pl.BlockSpec(memory_space=pl.ANY)
    dma = pltpu.SemaphoreType.DMA
    grad, table = pl.pallas_call(
        kernel,
        out_shape=(
            jax.ShapeDtypeStruct((12, 5120), F32),
            jax.ShapeDtypeStruct((192, 5120), BF16),
        ),
        in_specs=[hbm, hbm, vm, hbm, vm, vm, hbm, hbm, hbm],
        out_specs=(vm,) * 2,
        scratch_shapes=[
            pltpu.VMEM((192, 5120), BF16),
            pltpu.VMEM((12, 5120), F32),
            pltpu.VMEM((12, 5120), F32),
            pltpu.VMEM((12, 5120), F32),
            pltpu.VMEM((32, 160, 1024), BF16),
            pltpu.VMEM((192, 1024), BF16),
            pltpu.VMEM((NB, 4, 64, COLS), BF16),
            pltpu.VMEM((32, 64, COLS), BF16),
            pltpu.VMEM((8, UNITS, 4, HALF[0][1]), F32),
            pltpu.VMEM((8, UNITS, 4, HALF[1][1]), F32),
            pltpu.VMEM((8, UNITS, 4, HALF[0][1]), F32),
            pltpu.VMEM((8, UNITS, 4, HALF[1][1]), F32),
            pltpu.VMEM((NB, NY, NX, 3, 4, COLS), F32),
            pltpu.VMEM((NB, 2, 2, 3, 4, COLS), F32),
            pltpu.VMEM((NB, 2, 4, 3, 4, COLS), F32),
            pltpu.VMEM((NB, 4, 3, 4, COLS), F32),
            pltpu.VMEM((NB, 4, 3, 4, COLS), F32),
            pltpu.VMEM((NB, 3, 4, COLS), F32),
            pltpu.VMEM((2, NB, 3, 4, HALF[0][1]), F32),
            pltpu.VMEM((2, NB, 3, 4, HALF[1][1]), F32),
            pltpu.VMEM((256, COLS), F32),
            pltpu.VMEM((2, NY, NX, 3, 4, 4 * HALF[0][1]), BF16),
            pltpu.VMEM((2, NY, NX, 3, 4, 4 * HALF[1][1]), BF16),
            dma((2, 9, 2)), dma((2, 9, 2)), dma((2, 9, 2)), dma((2, 9, 2)),
            dma((2, 32)), dma((2, 32)), dma((2, 8, PARTS)), dma((2, 8, PARTS)),
            dma((NB, 2)), dma((NB, 2)), dma((NB, 2)), dma((NB, 2)), dma((NB, 4)), dma((NB, 4)),
            dma((2, DP)), dma((2, 2, NB)),
            dma((2, 2, 4)), dma((2, 2, 4)), dma((2, 2, 2)), dma((2, 2, 2)), dma((2, 2, 2)), dma((2, 2, 2)),
            dma((6,)),
        ],
        compiler_params=pltpu.CompilerParams(
            collective_id=0, has_side_effects=True, vmem_limit_bytes=60 * 1024 * 1024),
    )(hidden.T, logit_grad.T, predict_mask[None, :], slots, rows_in, slot_counts, master, first, second)
    return (*update(grad, master, first, second), table)


def solution(mesh):
    in_specs = (
        P("dp", "vocab"),
        P("dp", "vocab"),
        P("dp"),
        P(("dp", "vocab"), None, None, None),
        P(("dp", "vocab"), None, None),
        P(("dp", "vocab"), None),
        P(("vocab", "dp"), None),
        P(("vocab", "dp"), None),
        P(("vocab", "dp"), None),
    )
    out_specs = (
        P(("vocab", "dp"), None),
        P(("vocab", "dp"), None),
        P(("vocab", "dp"), None),
        P("vocab", None),
    )
    return jax.shard_map(local, mesh=mesh, in_specs=in_specs, out_specs=out_specs, check_vma=False)
```
